32 devices in a mesh: grp: 2 (over x), ev: 4 (over y, core), hd: 4 (over z).
Axes of the slice: x: 2, y: 2, z: 4, core: 2. Of those that a mesh axis runs over, the one named last changes fastest.
Arguments:
- hist_keys: bfloat16 [8, 16384, 1024], P('grp', 'ev', 'hd'), parts along dimension 0, may hold values from -6 to 6
- hist_values: bfloat16 [8, 16384, 1024], P('grp', 'ev', 'hd'), parts along dimension 0, may hold values from -6 to 6
- hist_len: int32 [8], P('grp'), parts along dimension 0, may hold values from 4096 to 16384
- new_queries: bfloat16 [8, 1024, 1024], P('grp', 'ev', 'hd'), parts along dimension 0, may hold values from -6 to 6
- event_gate: bfloat16 [8, 1024, 1024], P('grp', 'ev', 'hd'), parts along dimension 0, may hold values from -6 to 6
- key_weight: bfloat16 [1024, 1024], P(None, 'hd'), may hold values from -0.1875 to 0.1875
- value_weight: bfloat16 [1024, 1024], P(None, 'hd'), may hold values from -0.1875 to 0.1875
- event_gain: float32 [1024], P('hd'), may hold values from 0.25 to 1.75
- cand_queries: bfloat16 [4096, 1024], P(('grp', 'ev'), 'hd'), parts along dimension 0, may hold values from -6 to 6
- cand_gate: bfloat16 [4096, 1024], P(('grp', 'ev'), 'hd'), parts along dimension 0, may hold values from -6 to 6
- cand_gain: float32 [1024], P('hd'), may hold values from 0.25 to 1.75
- block_user: int32 [32], P(('grp', 'ev')), parts along dimension 0, may hold values from 0 to 3, as said below
- cand_count: int32 [8], P('grp'), parts along dimension 0, may hold values from 1 to 1024, as said below
Outputs:
- event_out: bfloat16 [8, 1024, 1024], P('grp', 'ev', 'hd'), parts along dimension 0
- cand_out: bfloat16 [4096, 1024], P(('grp', 'ev'), 'hd'), parts along dimension 0
The draws below stay inside these ranges and needn't reach their ends.
There are 2 independent parts, one for each index of `grp`. The reference program is written for one: setup_inputs(seed, part) draws one part's arguments, and reference() takes and returns one part's arrays. A program takes and returns all parts, laid end to end along the dimension named above; an argument that names none is the same for every part. Nothing has to cross between parts.
Inputs may be any that keep to these rules, and one draw needn't show every extreme that they name: `block_user`: blocks belong to users in order: the first ceil(cand_count[0] / 128) blocks to user 0, the next ceil(cand_count[1] / 128) to user 1, and so on; every user has at least one block and all 16 blocks are used. `cand_count`: the blocks of users add up to 16 as stated for block_user; one user has exactly 8 full blocks.
All inputs are finite; a program needn't handle non-finite values.
Results may differ from the reference program's by a relative error of at most 0.0072.
Values may be sent and summed in bfloat16 or wider, within the bound.
No kernel may reach another device: no remote copies, remote signals or barrier semaphores. Data moves between devices by JAX's collectives and lax.ppermute only.
A program may use at most 128 MiB of HBM per device.

```python
import jax
import jax.numpy as jnp
from jax import lax

USERS = 4
NEW = 1024
H = 8
HEAD = 128
D = 1024
HIST = 16384
BLOCK = 128
CANDS = 2048
NBLK = 16


def plan_blocks(key):
    busiest_blocks = NBLK // 2
    spare = NBLK - busiest_blocks - (USERS - 1)
    order = jax.random.permutation(jax.random.fold_in(key, 11), USERS).astype(jnp.int32)
    picks = jax.random.randint(jax.random.fold_in(key, 12), (spare,), 0, USERS - 1).astype(jnp.int32)
    owner = order[picks + 1]
    user_ids = jnp.arange(USERS, dtype=jnp.int32)
    is_busiest = (user_ids == order[0]).astype(jnp.int32)
    others = 1 + jnp.sum((owner[:, None] == user_ids[None, :]).astype(jnp.int32), axis=0)
    block_count = is_busiest * busiest_blocks + (1 - is_busiest) * others
    shortfall = jax.random.randint(jax.random.fold_in(key, 13), (USERS,), 0, BLOCK).astype(jnp.int32) * (1 - is_busiest)
    cand_total = (block_count * BLOCK - shortfall).astype(jnp.int32)
    ends = jnp.cumsum(block_count).astype(jnp.int32)
    block_ids = jnp.arange(NBLK, dtype=jnp.int32)
    block_owner = jnp.sum((block_ids[:, None] >= ends[None, :]).astype(jnp.int32), axis=1)
    return (block_owner.astype(jnp.int32), cand_total)


def draw_block_user(key, part):
    return plan_blocks(key)[0]


def draw_cand_count(key, part):
    return plan_blocks(key)[1]


def touch_ends(drawn, stream_key, low, high):
    spot = [jax.random.randint(jax.random.fold_in(stream_key, axis), (), 0, length) for axis, length in enumerate(drawn.shape)]
    widest = drawn.shape.index(max(drawn.shape))
    next_to = spot[:widest] + [(spot[widest] + 1) % drawn.shape[widest]] + spot[widest + 1:]
    return drawn.at[tuple(spot)].set(low).at[tuple(next_to)].set(high)


def block_scale(key, shape, split, low, top_value):
    def one(axis_at, parts):
        heights = jax.random.uniform(jax.random.fold_in(jax.random.fold_in(key, 6), axis_at), (parts,), jnp.float32, low / len(split), top_value / len(split))
        return jnp.repeat(jnp.exp(heights), shape[axis_at] // parts).reshape((-1,) + (1,) * (len(shape) - axis_at - 1))

    level = one(*split[0])
    for cut in split[1:]:
        level = level * one(*cut)
    return level


def noise(own_key, dims, scale, most, cuts=(), kind=jnp.bfloat16):
    entries = jax.random.normal(own_key, dims, jnp.float32) * scale
    if len(cuts) > 0:
        entries = block_scale(own_key, dims, cuts, -0.22, 0.18) * entries
    return jnp.clip(entries, min=-most, max=most).astype(kind)


def setup_inputs(seed: int = 0, part: int = 0) -> dict:
    key_list = jax.random.split(jax.random.key(seed), 14)
    own_keys = jax.random.split(jax.random.fold_in(key_list[13], part), 14)
    hist_keys = noise(own_keys[0], (USERS, HIST, D), 1.0, 6.0, ((1, 4), (2, 4)))
    hist_values = noise(own_keys[1], (USERS, HIST, D), 1.0, 6.0, ((1, 4), (2, 4)))
    hist_len = touch_ends(jax.random.randint(own_keys[2], (USERS,), HIST // 4, HIST + 1), jax.random.fold_in(own_keys[2], 1), HIST // 4, HIST).astype(jnp.int32)
    new_queries = noise(own_keys[3], (USERS, NEW, D), 1.0, 6.0, ((1, 4), (2, 4)))
    event_gate = noise(own_keys[4], (USERS, NEW, D), 1.0, 6.0, ((1, 4), (2, 4)))
    key_weight = noise(key_list[5], (D, D), D ** -0.5, 0.1875, ((1, 4),))
    value_weight = noise(key_list[6], (D, D), D ** -0.5, 0.1875, ((1, 4),))
    event_gain = jnp.clip(1.0 + 0.15 * jax.random.normal(key_list[7], (D,), jnp.float32), 0.25, 1.75)
    cand_queries = noise(own_keys[8], (CANDS, D), 1.0, 6.0, ((0, 4), (1, 4)))
    cand_gate = noise(own_keys[9], (CANDS, D), 1.0, 6.0, ((0, 4), (1, 4)))
    cand_gain = jnp.clip(1.0 + 0.15 * jax.random.normal(key_list[10], (D,), jnp.float32), 0.25, 1.75)
    block_user = draw_block_user(jax.random.fold_in(jax.random.fold_in(key_list[13], part), 71), part)
    cand_count = draw_cand_count(jax.random.fold_in(jax.random.fold_in(key_list[13], part), 71), part)
    return dict(hist_keys=hist_keys, hist_values=hist_values, hist_len=hist_len, new_queries=new_queries, event_gate=event_gate, key_weight=key_weight, value_weight=value_weight, event_gain=event_gain, cand_queries=cand_queries, cand_gate=cand_gate, cand_gain=cand_gain, block_user=block_user, cand_count=cand_count)


EPSILON = 1e-05

def head_norm(values, gain):
    centre = lax.optimization_barrier(jnp.mean(values, axis=-1, keepdims=True))
    shifted = values - centre
    spread = lax.optimization_barrier(jnp.mean(shifted * shifted, axis=-1, keepdims=True))
    return shifted * lax.rsqrt(spread + EPSILON) * gain

def reference(hist_keys, hist_values, hist_len, new_queries, event_gate, key_weight, value_weight, event_gain, cand_queries, cand_gate, cand_gain, block_user, cand_count):
    score_scale = HEAD ** (-0.5)
    key_block = min(1024, HIST)
    n_blocks = HIST // key_block
    queries_f = new_queries.astype(jnp.float32).reshape(USERS, NEW, H, HEAD)
    keys_split = hist_keys.reshape(USERS, n_blocks, key_block, H, HEAD)
    values_split = hist_values.reshape(USERS, n_blocks, key_block, H, HEAD)

    def history_step(total, block_idx):
        keys_here = lax.dynamic_index_in_dim(keys_split, block_idx, 1, keepdims=False).astype(jnp.float32)
        values_here = lax.dynamic_index_in_dim(values_split, block_idx, 1, keepdims=False).astype(jnp.float32)
        scores = jnp.einsum('unhd,ukhd->uhnk', queries_f, keys_here) * score_scale
        position = block_idx * key_block + jnp.arange(key_block, dtype=jnp.int32)
        alive = (position[None, :] < hist_len[:, None]).astype(jnp.float32)
        weights = (jax.nn.silu(scores) * alive[:, None, None, :]).astype(jnp.bfloat16)
        weights = lax.optimization_barrier(weights).astype(jnp.float32)
        return (total + jnp.einsum('uhnk,ukhd->unhd', weights, values_here), None)
    attended, _ = lax.scan(history_step, jnp.zeros((USERS, NEW, H, HEAD), jnp.float32), jnp.arange(n_blocks, dtype=jnp.int32))
    gate_e = event_gate.astype(jnp.float32).reshape(USERS, NEW, H, HEAD)
    event_out = (head_norm(attended, event_gain.reshape(H, HEAD)) * gate_e).astype(jnp.bfloat16).reshape(USERS, NEW, H * HEAD)
    flat = event_out.reshape(USERS * NEW, H * HEAD)
    fresh_keys = jnp.dot(flat, key_weight, preferred_element_type=jnp.float32).astype(jnp.bfloat16).reshape(USERS, NEW, H, HEAD)
    fresh_values = jnp.dot(flat, value_weight, preferred_element_type=jnp.float32).astype(jnp.bfloat16).reshape(USERS, NEW, H, HEAD)
    block_count = ((cand_count + BLOCK - 1) // BLOCK).astype(jnp.int32)
    first_block = jnp.cumsum(block_count).astype(jnp.int32) - block_count
    block_rank = jnp.arange(NBLK, dtype=jnp.int32) - first_block[block_user]
    limit = cand_count[block_user]
    cand_split = cand_queries.reshape(NBLK, BLOCK, H, HEAD)

    def candidate_block(items):
        block_query, owner = items
        keys_own = lax.dynamic_index_in_dim(fresh_keys, owner, 0, keepdims=False).astype(jnp.float32)
        values_own = lax.dynamic_index_in_dim(fresh_values, owner, 0, keepdims=False).astype(jnp.float32)
        scores = jnp.einsum('bhd,nhd->hbn', block_query.astype(jnp.float32), keys_own) * score_scale
        weights = jax.nn.silu(scores).astype(jnp.bfloat16)
        weights = lax.optimization_barrier(weights).astype(jnp.float32)
        return jnp.einsum('hbn,nhd->bhd', weights, values_own)
    cand_attn = lax.map(candidate_block, (cand_split, block_user))
    row_pos = block_rank[:, None] * BLOCK + jnp.arange(BLOCK, dtype=jnp.int32)[None, :]
    valid = (row_pos < limit[:, None]).astype(jnp.float32)
    gate_c = cand_gate.astype(jnp.float32).reshape(NBLK, BLOCK, H, HEAD)
    cand_out = (head_norm(cand_attn, cand_gain.reshape(H, HEAD)) * gate_c * valid[:, :, None, None]).astype(jnp.bfloat16).reshape(CANDS, H * HEAD)
    return (event_out, cand_out)
```

```python
import functools

import jax
import jax.numpy as jnp
from jax import lax
from jax.experimental import pallas as pl
from jax.experimental.pallas import tpu as pltpu
from jax.sharding import PartitionSpec as P

HEAD = 128
BLOCK = 128
EPSILON = 1e-05
SCALE = HEAD ** (-0.5)
HALF = 0.5 * SCALE
BF16 = jnp.bfloat16
F32 = jnp.float32


def qk(q, k):
    return lax.dot_general(q, k, (((1,), (1,)), ((), ())), preferred_element_type=F32)


def head_norm(values, gain):
    centre = jnp.mean(values, axis=-1, keepdims=True)
    shifted = values - centre
    spread = jnp.mean(shifted * shifted, axis=-1, keepdims=True)
    return shifted * lax.rsqrt(spread + EPSILON) * gain


def swap(x, axis, size, j):
    return lax.ppermute(x, axis, [(i, i ^ j) for i in range(size)])


def attend(user, q_list, odd, hist_len, place, keys, values):
    n = len(q_list)
    rows, width = q_list[0].shape
    hist_rows = keys.shape[1]
    tile = min(2048, hist_rows)
    steps = hist_rows // tile

    def kern(len_ref, place_ref, *refs):
        q_refs, (k_ref, v_ref), o_refs, acc = refs[:n], refs[n : n + 2], refs[n + 2 : 2 * n + 2], refs[-1]
        step = pl.program_id(1)
        left = len_ref[user] - place_ref[0] * hist_rows - step * tile

        @pl.when(step == 0)
        def _():
            acc[...] = jnp.zeros_like(acc)

        @pl.when(left > 0)
        def _():
            k = k_ref[0]
            row = lax.broadcasted_iota(jnp.int32, (tile, HEAD), 0)
            v = jnp.where(row < left, v_ref[0], jnp.zeros((tile, HEAD), BF16))
            for i in range(n):
                s = qk(q_refs[i][...], k).astype(BF16)
                w = s + s * jnp.tanh(s * BF16(HALF))
                acc[i] += jnp.dot(w, v, preferred_element_type=F32)

        @pl.when(step == steps - 1)
        def _():
            for i in range(n):
                o_refs[i][...] = (acc[i] * HALF).astype(o_refs[i].dtype)

    piece = pl.BlockSpec((rows, HEAD), lambda h, s, *_: (0, h))
    hist = pl.BlockSpec((1, tile, HEAD), lambda h, s, *_: (user, s, h))
    return pl.pallas_call(
        kern,
        grid_spec=pltpu.PrefetchScalarGridSpec(
            num_scalar_prefetch=2,
            grid=(width // HEAD, steps),
            in_specs=[piece] * n + [hist, hist],
            out_specs=[piece] * n,
            scratch_shapes=[pltpu.VMEM((n, rows, HEAD), F32)],
        ),
        out_shape=[jax.ShapeDtypeStruct((rows, width), BF16 if o else F32) for o in odd],
        name=f"attend{user}_{n}",
    )(hist_len, place, *q_list, keys, values)


def gate_events(user, parts, gain, gate):
    n = len(parts)
    rows, width = parts[0].shape

    def kern(*refs):
        p_refs, gain_ref, gate_ref, o_ref = refs[:n], refs[n], refs[n + 1], refs[n + 2]
        for h in range(width // HEAD):
            cols = slice(h * HEAD, (h + 1) * HEAD)
            total = p_refs[0][:, cols].astype(F32)
            for p in p_refs[1:]:
                total = total + p[:, cols].astype(F32)
            o_ref[:, cols] = (
                head_norm(total, gain_ref[:, cols]) * gate_ref[0, :, cols].astype(F32)
            ).astype(BF16)

    whole = pl.BlockSpec((rows, width), lambda i: (0, 0))
    return pl.pallas_call(
        kern,
        grid=(1,),
        in_specs=[whole] * n
        + [pl.BlockSpec((1, width), lambda i: (0, 0)), pl.BlockSpec((1, rows, width), lambda i: (user, 0, 0))],
        out_specs=whole,
        out_shape=jax.ShapeDtypeStruct((rows, width), BF16),
        name=f"gate{user}",
    )(*parts, gain, gate)


def project(user, n_users, pieces, column, key_weight, value_weight, fresh):
    n = len(pieces)
    rows, part = pieces[0].shape
    width = key_weight.shape[1]

    def kern(col_ref, *refs):
        p_refs, wk, wv = refs[:n], refs[n], refs[n + 1]
        k_ref, v_ref = refs[-2:]
        k = jnp.zeros((rows, width), F32)
        v = jnp.zeros((rows, width), F32)
        for j in range(n):
            from_row = pl.ds(pl.multiple_of((col_ref[0] ^ j) * part, part), part)
            k += jnp.dot(p_refs[j][...], wk[from_row, :], preferred_element_type=F32)
            v += jnp.dot(p_refs[j][...], wv[from_row, :], preferred_element_type=F32)
        k_ref[0] = k.astype(BF16)
        v_ref[0] = v.astype(BF16)

    full = lambda s: pl.BlockSpec(s, lambda i, *_: (0,) * len(s))
    slot = pl.BlockSpec((1, rows, width), lambda i, *_: (user, 0, 0))
    shape = jax.ShapeDtypeStruct((n_users, rows, width), BF16)
    extra = [] if fresh is None else list(fresh)
    return pl.pallas_call(
        kern,
        grid_spec=pltpu.PrefetchScalarGridSpec(
            num_scalar_prefetch=1,
            grid=(1,),
            in_specs=[full((rows, part))] * n
            + [full(key_weight.shape)] * 2
            + [pl.BlockSpec(memory_space=pl.ANY)] * len(extra),
            out_specs=[slot, slot],
        ),
        out_shape=[shape, shape],
        input_output_aliases={} if fresh is None else {n + 3: 0, n + 4: 1},
        name=f"project{user}",
    )(column, *pieces, key_weight, value_weight, *extra)


def user_of(block, count_ref, n_users):
    end = jnp.int32(0)
    user = jnp.int32(0)
    first = jnp.int32(0)
    for u in range(n_users - 1):
        end = end + lax.shift_right_logical(count_ref[u] + (BLOCK - 1), 7)
        past = block >= end
        user = jnp.where(past, u + 1, user)
        first = jnp.where(past, end, first)
    return user, first


def cand_sums(pieces, cand_count, place, keys, values):
    n = len(pieces)
    n_users, rows, width = keys.shape
    blocks = pieces[0].shape[0] // BLOCK

    def kern(count_ref, place_ref, *refs):
        q_refs, k_ref, v_ref, o_refs = refs[:n], refs[n], refs[n + 1], refs[n + 2 :]
        for j in range(n):
            for i in range(blocks):
                user, _ = user_of((place_ref[0] ^ j) * blocks + i, count_ref, n_users)
                for h in range(width // HEAD):
                    cols = slice(h * HEAD, (h + 1) * HEAD)
                    rws = slice(i * BLOCK, (i + 1) * BLOCK)
                    t = qk(q_refs[j][rws, cols], k_ref[user, :, cols]) * HALF
                    w = (t + t * jnp.tanh(t)).astype(BF16)
                    o = jnp.dot(w, v_ref[user, :, cols], preferred_element_type=F32)
                    o_refs[j][rws, cols] = o.astype(o_refs[j].dtype)

    full = lambda s: pl.BlockSpec(s, lambda i, *_: (0,) * len(s))
    piece = full(pieces[0].shape)
    return pl.pallas_call(
        kern,
        grid_spec=pltpu.PrefetchScalarGridSpec(
            num_scalar_prefetch=2,
            grid=(1,),
            in_specs=[piece] * n + [full(keys.shape)] * 2,
            out_specs=[piece] * n,
        ),
        out_shape=[jax.ShapeDtypeStruct(pieces[0].shape, BF16 if j & 1 else F32) for j in range(n)],
        name="cand_sums",
    )(cand_count, place, *pieces, keys, values)


def gate_cands(parts, cand_count, place, gain, gate):
    n = len(parts)
    n_users = cand_count.shape[0]
    rows, width = parts[0].shape

    def kern(count_ref, place_ref, *refs):
        p_refs, gain_ref, gate_ref, o_ref = refs[:n], refs[n], refs[n + 1], refs[n + 2]
        for i in range(rows // BLOCK):
            block = place_ref[0] * (rows // BLOCK) + i
            user, first = user_of(block, count_ref, n_users)
            limit = count_ref[user] - (block - first) * BLOCK
            live = lax.broadcasted_iota(jnp.int32, (BLOCK, HEAD), 0) < limit
            rws = slice(i * BLOCK, (i + 1) * BLOCK)
            for h in range(width // HEAD):
                cols = slice(h * HEAD, (h + 1) * HEAD)
                total = p_refs[0][rws, cols].astype(F32)
                for p in p_refs[1:]:
                    total = total + p[rws, cols].astype(F32)
                out = head_norm(total, gain_ref[:, cols]) * gate_ref[rws, cols].astype(F32)
                o_ref[rws, cols] = jnp.where(live, out, 0.0).astype(BF16)

    full = lambda s: pl.BlockSpec(s, lambda i, *_: (0,) * len(s))
    return pl.pallas_call(
        kern,
        grid_spec=pltpu.PrefetchScalarGridSpec(
            num_scalar_prefetch=2,
            grid=(1,),
            in_specs=[full((rows, width))] * n + [full((1, width)), full((rows, width))],
            out_specs=full((rows, width)),
        ),
        out_shape=jax.ShapeDtypeStruct((rows, width), BF16),
        name="gate_cands",
    )(cand_count, place, *parts, gain, gate)


def gather_pieces(x, axis, size):
    pieces = {0: x}
    for j in range(1, size):
        low = j & -j
        pieces[j] = None
    bit = size // 2
    while bit:
        for j in list(pieces):
            if pieces[j] is not None and pieces.get(j ^ bit, 0) is None:
                pieces[j ^ bit] = swap(pieces[j], axis, size, bit)
        bit //= 2
    return [pieces[j] for j in range(size)]


def scatter_sums(parts, axis, size):
    held = {j: [p] for j, p in enumerate(parts)}
    bit = 1
    while bit < size:
        for j in sorted(held):
            if j & bit:
                addends = held.pop(j)
                total = addends[0]
                if len(addends) > 1:
                    total = sum(a.astype(F32) for a in addends)
                held[j ^ bit].append(swap(total.astype(BF16), axis, size, bit))
        bit *= 2
    return held[0]


def make_local(n_ev, n_hd):
    def local(
        hist_keys,
        hist_values,
        hist_len,
        new_queries,
        event_gate,
        key_weight,
        value_weight,
        event_gain,
        cand_queries,
        cand_gate,
        cand_gain,
        block_user,
        cand_count,
    ):
        n_users, rows, width = new_queries.shape
        place = lax.axis_index("ev").astype(jnp.int32).reshape(1)
        column = lax.axis_index("hd").astype(jnp.int32).reshape(1)
        event_gain = event_gain.reshape(1, width)
        cand_gain = cand_gain.reshape(1, width)
        queries = [gather_pieces(new_queries[u], "ev", n_ev) for u in range(n_users)]
        cands = gather_pieces(cand_queries, "ev", n_ev)
        odd = [bool(j & 1) for j in range(n_ev)]
        event_out = []
        fresh = None
        for u in range(n_users):
            args = (hist_len, place, hist_keys, hist_values)
            if u == 0:
                parts = attend(u, queries[u][:1], odd[:1], *args)
                if n_ev > 1:
                    parts = parts + attend(u, queries[u][1:], odd[1:], *args)
            else:
                parts = attend(u, queries[u], odd, *args)
            gated = gate_events(u, scatter_sums(parts, "ev", n_ev), event_gain, event_gate)
            event_out.append(gated)
            pieces = [gated] + [swap(gated, "hd", n_hd, j) for j in range(1, n_hd)]
            fresh = project(u, n_users, pieces, column, key_weight, value_weight, fresh)
        sums = cand_sums(cands, cand_count, place, *fresh)
        cand_out = gate_cands(scatter_sums(sums, "ev", n_ev), cand_count, place, cand_gain, cand_gate)
        return jnp.stack(event_out), cand_out

    return local


def solution(mesh):
    return jax.shard_map(
        make_local(mesh.shape["ev"], mesh.shape["hd"]),
        mesh=mesh,
        in_specs=(
            P("grp", "ev", "hd"),
            P("grp", "ev", "hd"),
            P("grp"),
            P("grp", "ev", "hd"),
            P("grp", "ev", "hd"),
            P(None, "hd"),
            P(None, "hd"),
            P("hd"),
            P(("grp", "ev"), "hd"),
            P(("grp", "ev"), "hd"),
            P("hd"),
            P(("grp", "ev")),
            P("grp"),
        ),
        out_specs=(P("grp", "ev", "hd"), P(("grp", "ev"), "hd")),
        check_vma=False,
    )
```

```python
import jax
import jax.numpy as jnp
from jax import lax
from jax.experimental import pallas as pl
from jax.experimental.pallas import tpu as pltpu
from jax.sharding import PartitionSpec as P


HEAD = 128
BLOCK = 128
EPSILON = 1e-05
SCALE = HEAD ** (-0.5)
HALF = 0.5 * SCALE
BF16 = jnp.bfloat16
F32 = jnp.float32
ANY = pl.BlockSpec(memory_space=pl.ANY)


def qk(q, k):
    return lax.dot_general(q, k, (((1,), (1,)), ((), ())), preferred_element_type=F32)


def head_norm(values, gain):
    centre = jnp.mean(values, axis=-1, keepdims=True)
    shifted = values - centre
    spread = jnp.mean(shifted * shifted, axis=-1, keepdims=True)
    return shifted * lax.rsqrt(spread + EPSILON) * gain


def swap(x, axis, size, j):
    return lax.ppermute(x, axis, [(i, i ^ j) for i in range(size)])


def full(shape):
    return pl.BlockSpec(shape, lambda *_: (0,) * len(shape))


def attend(first_user, counts, half_rows, start, queries, own_first, hist_len, place, keys, values, after):
    n = len(queries)
    width = queries[0][0].shape[2]
    hist_rows = keys.shape[1]
    users = len(counts)
    take = max(counts)
    total = sum(counts) * half_rows
    group = max(1, 256 // (take * half_rows))
    n_after = len(after)

    def kern(len_ref, place_ref, *refs):
        q_refs, k_ref, v_ref = refs[:n], refs[n], refs[n + 1]
        o_refs = refs[n + 2 + n_after :]
        for g in range(users):
            rows = counts[g] * half_rows
            at = sum(counts[:g]) * half_rows

            def run(g=g, rows=rows, at=at):
                left = len_ref[first_user + g] - place_ref[0] * hist_rows

                @pl.when(left > 0)
                def _():
                    k = k_ref[0]
                    row = lax.broadcasted_iota(jnp.int32, (hist_rows, HEAD), 0)
                    v = jnp.where(row < left, v_ref[0], jnp.zeros((hist_rows, HEAD), BF16))
                    for i in range(0, n, group):
                        some = q_refs[i : i + group]
                        q = [r[0, :rows, :] for r in some]
                        q = q[0] if len(q) == 1 else jnp.concatenate(q, axis=0)
                        s = qk(q, k)
                        w = (s + s * jnp.tanh(s * HALF)).astype(BF16)
                        o = jnp.dot(w, v, preferred_element_type=F32) * HALF
                        for m, o_ref in enumerate(o_refs[i : i + group]):
                            o_ref[at : at + rows, :] = o[m * rows : (m + 1) * rows].astype(o_ref.dtype)

                @pl.when(left <= 0)
                def _():
                    for o_ref in o_refs:
                        o_ref[at : at + rows, :] = jnp.zeros((rows, HEAD), o_ref.dtype)

            if users == 1:
                run()
            else:
                pl.when(pl.program_id(1) == g)(run)

    def q_spec(offset):
        return pl.BlockSpec((1, take * half_rows, HEAD), lambda h, g, *_: (offset + g, start, h))

    hist = pl.BlockSpec((1, hist_rows, HEAD), lambda h, g, *_: (first_user + g, 0, h))
    kinds = [F32 if own_first and i == 0 else BF16 for i in range(n)]
    return pl.pallas_call(
        kern,
        grid_spec=pltpu.PrefetchScalarGridSpec(
            num_scalar_prefetch=2,
            grid=(width // HEAD, users),
            in_specs=[q_spec(off) for _, off in queries] + [hist, hist] + [ANY] * n_after,
            out_specs=[pl.BlockSpec((total, HEAD), lambda h, g, *_: (0, h))] * n,
        ),
        out_shape=[jax.ShapeDtypeStruct((total, width), kind) for kind in kinds],
        cost_estimate=pl.CostEstimate(
            flops=8 * n * total * hist_rows * width,
            transcendentals=n * total * hist_rows * width // HEAD,
            bytes_accessed=4 * users * hist_rows * width,
        ),
    )(hist_len, place, *[q for q, _ in queries], keys, values, *after)


def gate_events(own, own_at, others, tile, tiles, gate_at, gain, gate):
    n = len(others)
    width = own.shape[1]

    def kern(own_ref, *refs):
        p_refs, gain_ref, gate_ref, o_ref = refs[:n], refs[n], refs[n + 1], refs[n + 2]
        for h in range(width // HEAD):
            cols = slice(h * HEAD, (h + 1) * HEAD)
            total = own_ref[:, cols]
            for p in p_refs:
                total = total + p[:, cols].astype(F32)
            o_ref[:, cols] = (
                head_norm(total, gain_ref[:, cols]) * gate_ref[:, cols].astype(F32)
            ).astype(BF16)

    def at(offset):
        return pl.BlockSpec((tile, width), lambda i: (offset + i, 0))

    return pl.pallas_call(
        kern,
        grid=(tiles,),
        in_specs=[at(own_at)] + [at(0)] * n + [full((1, width)), at(gate_at)],
        out_specs=at(0),
        out_shape=jax.ShapeDtypeStruct((tile * tiles, width), BF16),
    )(own, *others, gain, gate)


def user_of(block, count_ref, n_users):
    end = jnp.int32(0)
    user = jnp.int32(0)
    first = jnp.int32(0)
    for u in range(n_users - 1):
        end = end + lax.shift_right_logical(count_ref[u] + (BLOCK - 1), 7)
        past = block >= end
        user = jnp.where(past, u + 1, user)
        first = jnp.where(past, end, first)
    return user, first


def cand_sums(users, n_users, chunks, cands, cand_count, place, column, key_weight, value_weight, earlier):
    n = len(cands)
    n_hd = len(chunks[0])
    part = chunks[0][0].shape[1]
    width = key_weight.shape[1]
    rows = sum(c[0].shape[0] for c in chunks) // len(users)
    blocks = cands[0].shape[0] // BLOCK
    flat = [p for c in chunks for p in c]
    lo, hi = users[0], users[-1]

    def kern(count_ref, place_ref, col_ref, *refs):
        e_refs = refs[: len(flat)]
        wk, wv = refs[len(flat) : len(flat) + 2]
        q_refs = refs[len(flat) + 2 : len(flat) + 2 + n]
        early = refs[len(flat) + 2 + n : -4]
        keep_ref, send_ref, k_ref, v_ref = refs[-4:]
        at = 0
        for c in range(len(chunks)):
            size = chunks[c][0].shape[0]
            k = jnp.zeros((size, width), F32)
            v = jnp.zeros((size, width), F32)
            for j in range(n_hd):
                from_row = pl.ds(pl.multiple_of((col_ref[0] ^ j) * part, part), part)
                e = e_refs[c * n_hd + j][...]
                k += jnp.dot(e, wk[from_row, :], preferred_element_type=F32)
                v += jnp.dot(e, wv[from_row, :], preferred_element_type=F32)
            k_ref[at : at + size, :] = k.astype(BF16)
            v_ref[at : at + size, :] = v.astype(BF16)
            at += size
        for j in range(n):
            o_ref = send_ref if j & 1 else keep_ref
            for i in range(blocks):
                user, _ = user_of((place_ref[0] ^ j) * blocks + i, count_ref, n_users)
                mine = (user >= lo) & (user <= hi)
                rws = slice(i * BLOCK, (i + 1) * BLOCK)

                @pl.when(mine)
                def _(j=j, o_ref=o_ref, user=user, rws=rws):
                    own = pl.ds(pl.multiple_of((user - lo) * rows, rows), rows)
                    for h in range(width // HEAD):
                        cols = slice(h * HEAD, (h + 1) * HEAD)
                        t = qk(q_refs[j][rws, cols], k_ref[own, cols]) * HALF
                        w = (t + t * jnp.tanh(t)).astype(BF16)
                        o = jnp.dot(w, v_ref[own, cols], preferred_element_type=F32)
                        o_ref[j // 2, rws, cols] = o.astype(o_ref.dtype)

                if early:

                    @pl.when(jnp.logical_not(mine))
                    def _(j=j, o_ref=o_ref, rws=rws):
                        o_ref[j // 2, rws, :] = early[j & 1][j // 2, rws, :]

    shape = (max(n // 2, 1), blocks * BLOCK, width)
    return pl.pallas_call(
        kern,
        grid_spec=pltpu.PrefetchScalarGridSpec(
            num_scalar_prefetch=3,
            grid=(1,),
            in_specs=[full(e.shape) for e in flat]
            + [full(key_weight.shape)] * 2
            + [full(c.shape) for c in cands]
            + [full(shape) for _ in earlier],
            out_specs=[full(shape)] * 2,
            scratch_shapes=[pltpu.VMEM((rows * len(users), width), BF16)] * 2,
        ),
        out_shape=[jax.ShapeDtypeStruct(shape, F32), jax.ShapeDtypeStruct(shape, BF16)],
    )(cand_count, place, column, *flat, key_weight, value_weight, *cands, *earlier)


def gate_cands(own, others, cand_count, place, gain, gate):
    n = 1 + len(others)
    n_users = cand_count.shape[0]
    rows, width = gate.shape

    def kern(count_ref, place_ref, *refs):
        p_refs, gain_ref, gate_ref, o_ref = refs[:n], refs[n], refs[n + 1], refs[n + 2]
        i = pl.program_id(0)
        block = place_ref[0] * (rows // BLOCK) + i
        user, first = user_of(block, count_ref, n_users)
        limit = count_ref[user] - (block - first) * BLOCK
        live = lax.broadcasted_iota(jnp.int32, (BLOCK, HEAD), 0) < limit
        for h in range(width // HEAD):
            cols = slice(h * HEAD, (h + 1) * HEAD)
            total = p_refs[0][0, :, cols].astype(F32)
            for p in p_refs[1:]:
                total = total + p[0, :, cols].astype(F32)
            out = head_norm(total, gain_ref[:, cols]) * gate_ref[:, cols].astype(F32)
            o_ref[:, cols] = jnp.where(live, out, 0.0).astype(BF16)

    part = pl.BlockSpec((1, BLOCK, width), lambda i, *_: (0, i, 0))
    block = pl.BlockSpec((BLOCK, width), lambda i, *_: (i, 0))
    return pl.pallas_call(
        kern,
        grid_spec=pltpu.PrefetchScalarGridSpec(
            num_scalar_prefetch=2,
            grid=(rows // BLOCK,),
            in_specs=[part] * n + [full((1, width)), block],
            out_specs=block,
        ),
        out_shape=jax.ShapeDtypeStruct((rows, width), BF16),
        name="gate_cands",
    )(cand_count, place, own, *others, gain, gate)


def gather_pieces(x, axis, size, skip=()):
    pieces = [x] + [None] * (size - 1)
    bit = size // 2
    while bit:
        for j in range(0, size, 2 * bit):
            if pieces[j] is not None and j + bit not in skip:
                pieces[j + bit] = swap(pieces[j], axis, size, bit)
        bit //= 2
    return pieces


def make_local(n_ev, n_hd):
    def local(
        hist_keys,
        hist_values,
        hist_len,
        new_queries,
        event_gate,
        key_weight,
        value_weight,
        event_gain,
        cand_queries,
        cand_gate,
        cand_gain,
        block_user,
        cand_count,
    ):
        n_users, rows, width = new_queries.shape
        half = rows // 2
        place = lax.axis_index("ev").astype(jnp.int32).reshape(1)
        column = lax.axis_index("hd").astype(jnp.int32).reshape(1)
        event_gain = event_gain.reshape(1, width)
        cand_gain = cand_gain.reshape(1, width)
        gates = event_gate.reshape(n_users * rows, width)
        early_q = gather_pieces(new_queries[:1], "ev", n_ev, skip=(1,))
        queries = gather_pieces(new_queries, "ev", n_ev)
        early_q[1] = queries[1]
        cands = gather_pieces(cand_queries, "ev", n_ev)
        hist = (hist_len, place, hist_keys, hist_values)

        own01 = attend(0, (2, 2), half, 0, [(new_queries, 0)], True, *hist, ())[0]

        def reduce(own, own_at, outs, tiles, gate_at):
            others = [swap(o, "ev", n_ev, j + 1) for j, o in enumerate(outs)]
            return gate_events(own, own_at, others, half, tiles, gate_at, event_gain, gates)


        out0 = attend(0, (2,), half, 0, [(q, 0) for q in early_q[1:]], False, *hist, (own01,))
        out1 = attend(1, (2,), half, 0, [(q, 1) for q in queries[1:]], False, *hist, (out0[0],))
        gated0 = reduce(own01, 0, out0, 2, 0)
        out2 = attend(2, (2, 1), half, 0, [(q, 2) for q in queries], True, *hist, (gated0, out1[0]))
        gated1 = reduce(own01, 2, out1, 2, 2)
        out3 = attend(3, (1,), half, 1, [(q, 3) for q in queries], True, *hist, (gated1, out2[0]))
        gated2 = reduce(out2[0], 0, out2[1:], 3, 4)
        gated3 = reduce(out3[0], 0, out3[1:], 1, 7)
        gated = [gated0, gated1, gated2, gated3]
        all_columns = [gather_pieces(g, "hd", n_hd) for g in gated]
        common = (cands, cand_count, place, column, key_weight, value_weight)
        first = cand_sums((0, 1), n_users, all_columns[:2], *common, ())
        keep, send = cand_sums((2, 3), n_users, all_columns[2:], *common, first)
        if n_ev == 1:
            cand_out = gate_cands(keep, [], cand_count, place, cand_gain, cand_gate)
        else:
            came = swap(send, "ev", n_ev, 1)
            bit = 2
            while bit < n_ev:
                total = keep + came.astype(F32)
                keep = total[0::2]
                came = swap(total[1::2].astype(BF16), "ev", n_ev, bit)
                bit *= 2
            cand_out = gate_cands(keep, [came], cand_count, place, cand_gain, cand_gate)
        event_out = jnp.concatenate(gated, axis=0)
        return event_out.reshape(n_users, rows, width), cand_out

    return local


def solution(mesh):
    return jax.shard_map(
        make_local(mesh.shape["ev"], mesh.shape["hd"]),
        mesh=mesh,
        in_specs=(
            P("grp", "ev", "hd"),
            P("grp", "ev", "hd"),
            P("grp"),
            P("grp", "ev", "hd"),
            P("grp", "ev", "hd"),
            P(None, "hd"),
            P(None, "hd"),
            P("hd"),
            P(("grp", "ev"), "hd"),
            P(("grp", "ev"), "hd"),
            P("hd"),
            P(("grp", "ev")),
            P("grp"),
        ),
        out_specs=(P("grp", "ev", "hd"), P(("grp", "ev"), "hd")),
        check_vma=False,
    )
```

```python
import jax
import jax.numpy as jnp
from jax import lax
from jax.experimental import pallas as pl
from jax.experimental.pallas import tpu as pltpu
from jax.sharding import PartitionSpec as P


HEAD = 128
BLOCK = 128
EPSILON = 1e-05
SCALE = HEAD ** (-0.5)
HALF = 0.5 * SCALE
BF16 = jnp.bfloat16
F32 = jnp.float32
ANY = pl.BlockSpec(memory_space=pl.ANY)


def qk(q, k):
    return lax.dot_general(q, k, (((1,), (1,)), ((), ())), preferred_element_type=F32)


def head_norm(values, gain):
    centre = jnp.mean(values, axis=-1, keepdims=True)
    shifted = values - centre
    spread = jnp.mean(shifted * shifted, axis=-1, keepdims=True)
    return shifted * lax.rsqrt(spread + EPSILON) * gain


def swap(x, axis, size, j):
    return lax.ppermute(x, axis, [(i, i ^ j) for i in range(size)])


def full(shape):
    return pl.BlockSpec(shape, lambda *_: (0,) * len(shape))


def attend(first_user, counts, half_rows, start, queries, own_first, hist_len, place, keys, values, after):
    n = len(queries)
    width = queries[0][0].shape[2]
    hist_rows = keys.shape[1]
    users = len(counts)
    take = max(counts)
    total = sum(counts) * half_rows
    n_after = len(after)

    def kern(len_ref, place_ref, *refs):
        q_refs, k_ref, v_ref = refs[:n], refs[n], refs[n + 1]
        o_refs = refs[n + 2 + n_after :]
        for g in range(users):
            rows = counts[g] * half_rows
            at = sum(counts[:g]) * half_rows

            def run(g=g, rows=rows, at=at):
                left = len_ref[first_user + g] - place_ref[0] * hist_rows

                @pl.when(left > 0)
                def _():
                    q = [r[0, :rows, :] for r in q_refs]
                    q = q[0] if n == 1 else jnp.concatenate(q, axis=0)
                    tile = min(hist_rows, 1024 if n * rows <= 256 else 256)
                    o = jnp.zeros((n * rows, HEAD), F32)
                    for t in range(0, hist_rows, tile):
                        row = t + lax.broadcasted_iota(jnp.int32, (tile, HEAD), 0)
                        v = jnp.where(row < left, v_ref[0, t : t + tile], jnp.zeros((tile, HEAD), BF16))
                        s = qk(q, k_ref[0, t : t + tile])
                        w = (s + s * jnp.tanh(s * HALF)).astype(BF16)
                        o = o + jnp.dot(w, v, preferred_element_type=F32)
                    o = o * HALF
                    for m, o_ref in enumerate(o_refs):
                        o_ref[at : at + rows, :] = o[m * rows : (m + 1) * rows].astype(o_ref.dtype)

                @pl.when(left <= 0)
                def _():
                    for o_ref in o_refs:
                        o_ref[at : at + rows, :] = jnp.zeros((rows, HEAD), o_ref.dtype)

            if users == 1:
                run()
            else:
                pl.when(pl.program_id(1) == g)(run)

    def q_spec(offset):
        return pl.BlockSpec((1, take * half_rows, HEAD), lambda h, g, *_: (offset + g, start, h))

    hist = pl.BlockSpec((1, hist_rows, HEAD), lambda h, g, *_: (first_user + g, 0, h))
    kinds = [F32 if own_first and i == 0 else BF16 for i in range(n)]
    return pl.pallas_call(
        kern,
        grid_spec=pltpu.PrefetchScalarGridSpec(
            num_scalar_prefetch=2,
            grid=(width // HEAD, users),
            in_specs=[q_spec(off) for _, off in queries] + [hist, hist] + [ANY] * n_after,
            out_specs=[pl.BlockSpec((total, HEAD), lambda h, g, *_: (0, h))] * n,
        ),
        out_shape=[jax.ShapeDtypeStruct((total, width), kind) for kind in kinds],
        cost_estimate=pl.CostEstimate(
            flops=8 * n * total * hist_rows * width,
            transcendentals=n * total * hist_rows * width // HEAD,
            bytes_accessed=4 * users * hist_rows * width,
        ),
    )(hist_len, place, *[q for q, _ in queries], keys, values, *after)


def gate_events(own, own_at, others, rows, gate_at, gain, gate):
    n = len(others)
    width = own.shape[1]

    def kern(own_ref, *refs):
        p_refs, gain_ref, gate_ref, o_ref = refs[:n], refs[n], refs[n + 1], refs[n + 2]
        for h in range(width // HEAD):
            cols = slice(h * HEAD, (h + 1) * HEAD)
            total = own_ref[:, cols]
            for p in p_refs:
                total = total + p[:, cols].astype(F32)
            o_ref[:, cols] = (
                head_norm(total, gain_ref[:, cols]) * gate_ref[:, cols].astype(F32)
            ).astype(BF16)

    def at(offset):
        return pl.BlockSpec((pl.Element(rows), pl.Element(width)), lambda i: (offset, 0))

    return pl.pallas_call(
        kern,
        grid=(1,),
        in_specs=[at(own_at)] + [full((rows, width))] * n + [full((1, width)), at(gate_at)],
        out_specs=full((rows, width)),
        out_shape=jax.ShapeDtypeStruct((rows, width), BF16),
    )(own, *others, gain, gate)


def user_of(block, count_ref, n_users):
    end = jnp.int32(0)
    user = jnp.int32(0)
    first = jnp.int32(0)
    for u in range(n_users - 1):
        end = end + lax.shift_right_logical(count_ref[u] + (BLOCK - 1), 7)
        past = block >= end
        user = jnp.where(past, u + 1, user)
        first = jnp.where(past, end, first)
    return user, first


def project(e_refs, n_hd, sizes, col_ref, wk, wv, k_ref, v_ref, at):
    part = wk.shape[0] // n_hd
    for c, size in enumerate(sizes):
        k = jnp.zeros((size, wk.shape[1]), F32)
        v = jnp.zeros((size, wk.shape[1]), F32)
        for j in range(n_hd):
            from_row = pl.ds(pl.multiple_of((col_ref[0] ^ j) * part, part), part)
            e = e_refs[c * n_hd + j][...]
            k += jnp.dot(e, wk[from_row, :], preferred_element_type=F32)
            v += jnp.dot(e, wv[from_row, :], preferred_element_type=F32)
        k_ref[at : at + size, :] = k.astype(BF16)
        v_ref[at : at + size, :] = v.astype(BF16)
        at += size


def early_keys(chunks, column, key_weight, value_weight):
    n_hd = len(chunks[0])
    flat = [p for c in chunks for p in c]
    sizes = [c[0].shape[0] for c in chunks]
    shape = (sum(sizes), key_weight.shape[1])

    def kern(col_ref, *refs):
        project(refs[: len(flat)], n_hd, sizes, col_ref, *refs[len(flat) :], 0)

    return pl.pallas_call(
        kern,
        grid_spec=pltpu.PrefetchScalarGridSpec(
            num_scalar_prefetch=1,
            grid=(1,),
            in_specs=[full(e.shape) for e in flat] + [full(key_weight.shape)] * 2,
            out_specs=[full(shape)] * 2,
        ),
        out_shape=[jax.ShapeDtypeStruct(shape, BF16)] * 2,
        name="early_keys",
    )(column, *flat, key_weight, value_weight)


def cand_sums(n_users, early, chunks, cands, cand_count, place, column, key_weight, value_weight):
    n = len(cands)
    n_hd = len(chunks[0])
    width = key_weight.shape[1]
    flat = [p for c in chunks for p in c]
    sizes = [c[0].shape[0] for c in chunks]
    done = early[0].shape[0]
    rows = (done + sum(sizes)) // n_users
    blocks = cands[0].shape[0] // BLOCK

    def kern(count_ref, place_ref, col_ref, *refs):
        e_refs, refs = refs[: len(flat)], refs[len(flat) :]
        wk, wv, early_k, early_v = refs[:4]
        q_refs = refs[4 : 4 + n]
        keep_ref, send_ref, k_ref, v_ref = refs[-4:]
        k_ref[:done, :] = early_k[...]
        v_ref[:done, :] = early_v[...]
        project(e_refs, n_hd, sizes, col_ref, wk, wv, k_ref, v_ref, done)
        for j in range(n):
            o_ref = send_ref if j & 1 else keep_ref
            for i in range(blocks):
                user, _ = user_of((place_ref[0] ^ j) * blocks + i, count_ref, n_users)
                rws = slice(i * BLOCK, (i + 1) * BLOCK)
                own = pl.ds(pl.multiple_of(user * rows, rows), rows)
                for h in range(width // HEAD):
                    cols = slice(h * HEAD, (h + 1) * HEAD)
                    t = qk(q_refs[j][rws, cols], k_ref[own, cols]) * HALF
                    w = (t + t * jnp.tanh(t)).astype(BF16)
                    o = jnp.dot(w, v_ref[own, cols], preferred_element_type=F32)
                    o_ref[j // 2, rws, cols] = o.astype(o_ref.dtype)

    shape = (max(n // 2, 1), blocks * BLOCK, width)
    return pl.pallas_call(
        kern,
        grid_spec=pltpu.PrefetchScalarGridSpec(
            num_scalar_prefetch=3,
            grid=(1,),
            in_specs=[full(e.shape) for e in flat]
            + [full(key_weight.shape)] * 2
            + [full(early[0].shape)] * 2
            + [full(c.shape) for c in cands],
            out_specs=[full(shape)] * 2,
            scratch_shapes=[pltpu.VMEM((rows * n_users, width), BF16)] * 2,
        ),
        out_shape=[jax.ShapeDtypeStruct(shape, F32), jax.ShapeDtypeStruct(shape, BF16)],
        name="cand_sums",
    )(cand_count, place, column, *flat, key_weight, value_weight, *early, *cands)


def gate_cands(own, others, cand_count, place, gain, gate):
    n = 1 + len(others)
    n_users = cand_count.shape[0]
    rows, width = gate.shape

    def kern(count_ref, place_ref, *refs):
        p_refs, gain_ref, gate_ref, o_ref = refs[:n], refs[n], refs[n + 1], refs[n + 2]
        for i in range(rows // BLOCK):
            rws = slice(i * BLOCK, (i + 1) * BLOCK)
            block = place_ref[0] * (rows // BLOCK) + i
            user, first = user_of(block, count_ref, n_users)
            limit = count_ref[user] - (block - first) * BLOCK
            live = lax.broadcasted_iota(jnp.int32, (BLOCK, HEAD), 0) < limit
            for h in range(width // HEAD):
                cols = slice(h * HEAD, (h + 1) * HEAD)
                total = p_refs[0][0, rws, cols].astype(F32)
                for p in p_refs[1:]:
                    total = total + p[0, rws, cols].astype(F32)
                out = head_norm(total, gain_ref[:, cols]) * gate_ref[rws, cols].astype(F32)
                o_ref[rws, cols] = jnp.where(live, out, 0.0).astype(BF16)

    part = pl.BlockSpec((1, rows, width), lambda i, *_: (0, 0, 0))
    block = full((rows, width))
    return pl.pallas_call(
        kern,
        grid_spec=pltpu.PrefetchScalarGridSpec(
            num_scalar_prefetch=2,
            grid=(1,),
            in_specs=[part] * n + [full((1, width)), block],
            out_specs=block,
        ),
        out_shape=jax.ShapeDtypeStruct((rows, width), BF16),
        name="gate_cands",
    )(cand_count, place, own, *others, gain, gate)


def gather_pieces(x, axis, size, skip=()):
    pieces = [x] + [None] * (size - 1)
    bit = size // 2
    while bit:
        for j in range(0, size, 2 * bit):
            if pieces[j] is not None and j + bit not in skip:
                pieces[j + bit] = swap(pieces[j], axis, size, bit)
        bit //= 2
    return pieces


def make_local(n_ev, n_hd):
    def local(
        hist_keys,
        hist_values,
        hist_len,
        new_queries,
        event_gate,
        key_weight,
        value_weight,
        event_gain,
        cand_queries,
        cand_gate,
        cand_gain,
        block_user,
        cand_count,
    ):
        n_users, rows, width = new_queries.shape
        half = rows // 2
        place = lax.axis_index("ev").astype(jnp.int32).reshape(1)
        column = lax.axis_index("hd").astype(jnp.int32).reshape(1)
        event_gain = event_gain.reshape(1, width)
        cand_gain = cand_gain.reshape(1, width)
        gates = event_gate.reshape(n_users * rows, width)
        early_q = gather_pieces(new_queries[:1], "ev", n_ev, skip=(1,))
        queries = gather_pieces(new_queries, "ev", n_ev)
        early_q[1] = queries[1]
        cands = gather_pieces(cand_queries, "ev", n_ev)
        hist = (hist_len, place, hist_keys, hist_values)

        own01 = attend(0, (2, 2), half, 0, [(new_queries, 0)], True, *hist, ())[0]

        def reduce(own, own_at, outs, halves, gate_at):
            others = [swap(o, "ev", n_ev, j + 1) for j, o in enumerate(outs)]
            return gate_events(own, own_at * half, others, halves * half, gate_at * half, event_gain, gates)


        out0 = attend(0, (2,), half, 0, [(q, 0) for q in early_q[1:]], False, *hist, (own01,))
        out1 = attend(1, (2,), half, 0, [(q, 1) for q in queries[1:]], False, *hist, (out0[0],))
        gated0 = reduce(own01, 0, out0, 2, 0)
        out2 = attend(2, (2, 1), half, 0, [(q, 2) for q in queries], True, *hist, (gated0, out1[0]))
        gated1 = reduce(own01, 2, out1, 2, 2)
        out3 = attend(3, (1,), half, 1, [(q, 3) for q in queries], True, *hist, (gated1, out2[0]))
        gated2 = reduce(out2[0], 0, out2[1:], 3, 4)
        gated3 = reduce(out3[0], 0, out3[1:], 1, 7)
        gated = [gated0, gated1, gated2, gated3]
        all_columns = [gather_pieces(g, "hd", n_hd) for g in gated]
        early = early_keys(all_columns[:2], column, key_weight, value_weight)
        keep, send = cand_sums(
            n_users, early, all_columns[2:], cands, cand_count, place, column, key_weight, value_weight
        )
        if n_ev == 1:
            cand_out = gate_cands(keep, [], cand_count, place, cand_gain, cand_gate)
        else:
            came = swap(send, "ev", n_ev, 1)
            bit = 2
            while bit < n_ev:
                total = keep + came.astype(F32)
                keep = total[0::2]
                came = swap(total[1::2].astype(BF16), "ev", n_ev, bit)
                bit *= 2
            cand_out = gate_cands(keep, [came], cand_count, place, cand_gain, cand_gate)
        event_out = jnp.concatenate(gated, axis=0)
        return event_out.reshape(n_users, rows, width), cand_out

    return local


def solution(mesh):
    return jax.shard_map(
        make_local(mesh.shape["ev"], mesh.shape["hd"]),
        mesh=mesh,
        in_specs=(
            P("grp", "ev", "hd"),
            P("grp", "ev", "hd"),
            P("grp"),
            P("grp", "ev", "hd"),
            P("grp", "ev", "hd"),
            P(None, "hd"),
            P(None, "hd"),
            P("hd"),
            P(("grp", "ev"), "hd"),
            P(("grp", "ev"), "hd"),
            P("hd"),
            P(("grp", "ev")),
            P("grp"),
        ),
        out_specs=(P("grp", "ev", "hd"), P(("grp", "ev"), "hd")),
        check_vma=False,
    )
```

```python
import jax
import jax.numpy as jnp
from jax import lax
from jax.experimental import pallas as pl
from jax.experimental.pallas import tpu as pltpu
from jax.sharding import PartitionSpec as P


HEAD = 128
BLOCK = 128
EPSILON = 1e-05
SCALE = HEAD ** (-0.5)
HALF = 0.5 * SCALE
BF16 = jnp.bfloat16
F32 = jnp.float32
ANY = pl.BlockSpec(memory_space=pl.ANY)
SMALL = pltpu.CompilerParams(vmem_limit_bytes=12 << 20)
LARGE = pltpu.CompilerParams(vmem_limit_bytes=20 << 20)


def qk(q, k):
    return lax.dot_general(q, k, (((1,), (1,)), ((), ())), preferred_element_type=F32)


def head_norm(values, gain):
    centre = jnp.mean(values, axis=-1, keepdims=True)
    shifted = values - centre
    spread = jnp.mean(shifted * shifted, axis=-1, keepdims=True)
    return shifted * lax.rsqrt(spread + EPSILON) * gain


def swap(x, axis, size, j):
    return lax.ppermute(x, axis, [(i, i ^ j) for i in range(size)])


def full(shape):
    return pl.BlockSpec(shape, lambda *_: (0,) * len(shape))


def attend(first_user, counts, half_rows, start, queries, own_first, hist_len, place, keys, values, after):
    n = len(queries)
    width = queries[0][0].shape[2]
    hist_rows = keys.shape[1]
    users = len(counts)
    take = max(counts)
    total = sum(counts) * half_rows
    n_after = len(after)

    def kern(len_ref, place_ref, *refs):
        q_refs, k_ref, v_ref = refs[:n], refs[n], refs[n + 1]
        o_refs = refs[n + 2 + n_after :]
        for g in range(users):
            rows = counts[g] * half_rows
            at = sum(counts[:g]) * half_rows

            def run(g=g, rows=rows, at=at):
                left = len_ref[first_user + g] - place_ref[0] * hist_rows

                @pl.when(left > 0)
                def _():
                    q = [r[0, :rows, :] for r in q_refs]
                    q = q[0] if n == 1 else jnp.concatenate(q, axis=0)
                    tile = min(hist_rows, 1024 if n * rows <= 256 else 256)
                    o = jnp.zeros((n * rows, HEAD), F32)
                    for t in range(0, hist_rows, tile):
                        row = t + lax.broadcasted_iota(jnp.int32, (tile, HEAD), 0)
                        v = jnp.where(row < left, v_ref[0, t : t + tile], jnp.zeros((tile, HEAD), BF16))
                        s = qk(q, k_ref[0, t : t + tile])
                        w = (s + s * jnp.tanh(s * HALF)).astype(BF16)
                        o = o + jnp.dot(w, v, preferred_element_type=F32)
                    o = o * HALF
                    for m, o_ref in enumerate(o_refs):
                        o_ref[at : at + rows, :] = o[m * rows : (m + 1) * rows].astype(o_ref.dtype)

                @pl.when(left <= 0)
                def _():
                    for o_ref in o_refs:
                        o_ref[at : at + rows, :] = jnp.zeros((rows, HEAD), o_ref.dtype)

            if users == 1:
                run()
            else:
                pl.when(pl.program_id(1) == g)(run)

    def q_spec(offset):
        return pl.BlockSpec((1, take * half_rows, HEAD), lambda h, g, *_: (offset + g, start, h))

    hist = pl.BlockSpec((1, hist_rows, HEAD), lambda h, g, *_: (first_user + g, 0, h))
    kinds = [F32 if own_first and i == 0 else BF16 for i in range(n)]
    return pl.pallas_call(
        kern,
        grid_spec=pltpu.PrefetchScalarGridSpec(
            num_scalar_prefetch=2,
            grid=(width // HEAD, users),
            in_specs=[q_spec(off) for _, off in queries] + [hist, hist] + [ANY] * n_after,
            out_specs=[pl.BlockSpec((total, HEAD), lambda h, g, *_: (0, h))] * n,
        ),
        out_shape=[jax.ShapeDtypeStruct((total, width), kind) for kind in kinds],
        cost_estimate=pl.CostEstimate(
            flops=8 * n * total * hist_rows * width,
            transcendentals=n * total * hist_rows * width // HEAD,
            bytes_accessed=4 * users * hist_rows * width,
        ),
        compiler_params=LARGE,
    )(hist_len, place, *[q for q, _ in queries], keys, values, *after)


def gate_events(own, own_at, others, rows, gate_at, gain, gate):
    n = len(others)
    width = own.shape[1]

    def kern(own_ref, *refs):
        p_refs, gain_ref, gate_ref, o_ref = refs[:n], refs[n], refs[n + 1], refs[n + 2]
        for h in range(width // HEAD):
            cols = slice(h * HEAD, (h + 1) * HEAD)
            total = own_ref[:, cols]
            for p in p_refs:
                total = total + p[:, cols].astype(F32)
            o_ref[:, cols] = (
                head_norm(total, gain_ref[:, cols]) * gate_ref[:, cols].astype(F32)
            ).astype(BF16)

    def at(offset):
        return pl.BlockSpec((pl.Element(rows), pl.Element(width)), lambda i: (offset, 0))

    return pl.pallas_call(
        kern,
        grid=(1,),
        in_specs=[at(own_at)] + [full((rows, width))] * n + [full((1, width)), at(gate_at)],
        out_specs=full((rows, width)),
        out_shape=jax.ShapeDtypeStruct((rows, width), BF16),
        compiler_params=SMALL,
    )(own, *others, gain, gate)


def user_of(block, count_ref, n_users):
    end = jnp.int32(0)
    user = jnp.int32(0)
    first = jnp.int32(0)
    for u in range(n_users - 1):
        end = end + lax.shift_right_logical(count_ref[u] + (BLOCK - 1), 7)
        past = block >= end
        user = jnp.where(past, u + 1, user)
        first = jnp.where(past, end, first)
    return user, first


def project(e_refs, n_hd, sizes, col_ref, wk, wv, k_ref, v_ref, at):
    part = wk.shape[0] // n_hd
    for c, size in enumerate(sizes):
        k = jnp.zeros((size, wk.shape[1]), F32)
        v = jnp.zeros((size, wk.shape[1]), F32)
        for j in range(n_hd):
            from_row = pl.ds(pl.multiple_of((col_ref[0] ^ j) * part, part), part)
            e = e_refs[c * n_hd + j][...]
            k += jnp.dot(e, wk[from_row, :], preferred_element_type=F32)
            v += jnp.dot(e, wv[from_row, :], preferred_element_type=F32)
        k_ref[at : at + size, :] = k.astype(BF16)
        v_ref[at : at + size, :] = v.astype(BF16)
        at += size


def early_keys(chunks, column, key_weight, value_weight):
    n_hd = len(chunks[0])
    flat = [p for c in chunks for p in c]
    sizes = [c[0].shape[0] for c in chunks]
    shape = (sum(sizes), key_weight.shape[1])

    def kern(col_ref, *refs):
        project(refs[: len(flat)], n_hd, sizes, col_ref, *refs[len(flat) :], 0)

    return pl.pallas_call(
        kern,
        grid_spec=pltpu.PrefetchScalarGridSpec(
            num_scalar_prefetch=1,
            grid=(1,),
            in_specs=[full(e.shape) for e in flat] + [full(key_weight.shape)] * 2,
            out_specs=[full(shape)] * 2,
        ),
        out_shape=[jax.ShapeDtypeStruct(shape, BF16)] * 2,
        compiler_params=SMALL,
        name="early_keys",
    )(column, *flat, key_weight, value_weight)


def cand_sums(n_users, early, chunks, cands, cand_count, place, column, key_weight, value_weight):
    n = len(cands)
    n_hd = len(chunks[0])
    width = key_weight.shape[1]
    flat = [p for c in chunks for p in c]
    sizes = [c[0].shape[0] for c in chunks]
    done = early[0].shape[0]
    rows = (done + sum(sizes)) // n_users
    blocks = cands[0].shape[0] // BLOCK

    def kern(count_ref, place_ref, col_ref, *refs):
        e_refs, refs = refs[: len(flat)], refs[len(flat) :]
        wk, wv, early_k, early_v = refs[:4]
        q_refs = refs[4 : 4 + n]
        keep_ref, send_ref, k_ref, v_ref = refs[-4:]
        k_ref[:done, :] = early_k[...]
        v_ref[:done, :] = early_v[...]
        project(e_refs, n_hd, sizes, col_ref, wk, wv, k_ref, v_ref, done)
        for j in range(n):
            o_ref = send_ref if j & 1 else keep_ref
            for i in range(blocks):
                user, _ = user_of((place_ref[0] ^ j) * blocks + i, count_ref, n_users)
                rws = slice(i * BLOCK, (i + 1) * BLOCK)
                own = pl.ds(pl.multiple_of(user * rows, rows), rows)
                for h in range(width // HEAD):
                    cols = slice(h * HEAD, (h + 1) * HEAD)
                    t = qk(q_refs[j][rws, cols], k_ref[own, cols]) * HALF
                    w = (t + t * jnp.tanh(t)).astype(BF16)
                    o = jnp.dot(w, v_ref[own, cols], preferred_element_type=F32)
                    o_ref[j // 2, rws, cols] = o.astype(o_ref.dtype)

    shape = (max(n // 2, 1), blocks * BLOCK, width)
    return pl.pallas_call(
        kern,
        grid_spec=pltpu.PrefetchScalarGridSpec(
            num_scalar_prefetch=3,
            grid=(1,),
            in_specs=[full(e.shape) for e in flat]
            + [full(key_weight.shape)] * 2
            + [full(early[0].shape)] * 2
            + [full(c.shape) for c in cands],
            out_specs=[full(shape)] * 2,
            scratch_shapes=[pltpu.VMEM((rows * n_users, width), BF16)] * 2,
        ),
        out_shape=[jax.ShapeDtypeStruct(shape, F32), jax.ShapeDtypeStruct(shape, BF16)],
        compiler_params=SMALL,
        name="cand_sums",
    )(cand_count, place, column, *flat, key_weight, value_weight, *early, *cands)


def gate_cands(own, others, cand_count, place, gain, gate):
    n = 1 + len(others)
    n_users = cand_count.shape[0]
    rows, width = gate.shape

    def kern(count_ref, place_ref, *refs):
        p_refs, gain_ref, gate_ref, o_ref = refs[:n], refs[n], refs[n + 1], refs[n + 2]
        for i in range(rows // BLOCK):
            rws = slice(i * BLOCK, (i + 1) * BLOCK)
            block = place_ref[0] * (rows // BLOCK) + i
            user, first = user_of(block, count_ref, n_users)
            limit = count_ref[user] - (block - first) * BLOCK
            live = lax.broadcasted_iota(jnp.int32, (BLOCK, HEAD), 0) < limit
            for h in range(width // HEAD):
                cols = slice(h * HEAD, (h + 1) * HEAD)
                total = p_refs[0][0, rws, cols].astype(F32)
                for p in p_refs[1:]:
                    total = total + p[0, rws, cols].astype(F32)
                out = head_norm(total, gain_ref[:, cols]) * gate_ref[rws, cols].astype(F32)
                o_ref[rws, cols] = jnp.where(live, out, 0.0).astype(BF16)

    part = pl.BlockSpec((1, rows, width), lambda i, *_: (0, 0, 0))
    block = full((rows, width))
    return pl.pallas_call(
        kern,
        grid_spec=pltpu.PrefetchScalarGridSpec(
            num_scalar_prefetch=2,
            grid=(1,),
            in_specs=[part] * n + [full((1, width)), block],
            out_specs=block,
        ),
        out_shape=jax.ShapeDtypeStruct((rows, width), BF16),
        compiler_params=SMALL,
        name="gate_cands",
    )(cand_count, place, own, *others, gain, gate)


def gather_pieces(x, axis, size, skip=()):
    pieces = [x] + [None] * (size - 1)
    bit = size // 2
    while bit:
        for j in range(0, size, 2 * bit):
            if pieces[j] is not None and j + bit not in skip:
                pieces[j + bit] = swap(pieces[j], axis, size, bit)
        bit //= 2
    return pieces


def make_local(n_ev, n_hd):
    def local(
        hist_keys,
        hist_values,
        hist_len,
        new_queries,
        event_gate,
        key_weight,
        value_weight,
        event_gain,
        cand_queries,
        cand_gate,
        cand_gain,
        block_user,
        cand_count,
    ):
        n_users, rows, width = new_queries.shape
        half = rows // 2
        place = lax.axis_index("ev").astype(jnp.int32).reshape(1)
        column = lax.axis_index("hd").astype(jnp.int32).reshape(1)
        event_gain = event_gain.reshape(1, width)
        cand_gain = cand_gain.reshape(1, width)
        gates = event_gate.reshape(n_users * rows, width)
        new_in_hbm, *kv_in_hbm = [
            pltpu.with_memory_space_constraint(x, pltpu.HBM) for x in (new_queries, hist_keys, hist_values)
        ]
        early_q = gather_pieces(new_queries[:1], "ev", n_ev, skip=(1,))
        queries = gather_pieces(new_queries, "ev", n_ev)
        early_q[1] = queries[1]
        queries[0] = new_in_hbm
        cands = gather_pieces(cand_queries, "ev", n_ev)
        hist = (hist_len, place, *kv_in_hbm)

        own01 = attend(0, (2, 2), half, 0, [(new_in_hbm, 0)], True, *hist, ())[0]

        def reduce(own, own_at, outs, halves, gate_at):
            others = [swap(o, "ev", n_ev, j + 1) for j, o in enumerate(outs)]
            return gate_events(own, own_at * half, others, halves * half, gate_at * half, event_gain, gates)


        out0 = attend(0, (2,), half, 0, [(q, 0) for q in early_q[1:]], False, *hist, (own01,))
        out1 = attend(1, (2,), half, 0, [(q, 1) for q in queries[1:]], False, *hist, (out0[0],))
        gated0 = reduce(own01, 0, out0, 2, 0)
        out2 = attend(2, (2, 1), half, 0, [(q, 2) for q in queries], True, *hist, (gated0, out1[0]))
        gated1 = reduce(own01, 2, out1, 2, 2)
        out3 = attend(3, (1,), half, 1, [(q, 3) for q in queries], True, *hist, (gated1, out2[0]))
        gated2 = reduce(out2[0], 0, out2[1:], 3, 4)
        gated3 = reduce(out3[0], 0, out3[1:], 1, 7)
        gated = [gated0, gated1, gated2, gated3]
        all_columns = [gather_pieces(g, "hd", n_hd) for g in gated]
        early = early_keys(all_columns[:2], column, key_weight, value_weight)
        keep, send = cand_sums(
            n_users, early, all_columns[2:], cands, cand_count, place, column, key_weight, value_weight
        )
        if n_ev == 1:
            cand_out = gate_cands(keep, [], cand_count, place, cand_gain, cand_gate)
        else:
            came = swap(send, "ev", n_ev, 1)
            bit = 2
            while bit < n_ev:
                total = keep + came.astype(F32)
                keep = total[0::2]
                came = swap(total[1::2].astype(BF16), "ev", n_ev, bit)
                bit *= 2
            cand_out = gate_cands(keep, [came], cand_count, place, cand_gain, cand_gate)
        event_out = jnp.concatenate(gated, axis=0)
        return event_out.reshape(n_users, rows, width), cand_out

    return local


def solution(mesh):
    return jax.shard_map(
        make_local(mesh.shape["ev"], mesh.shape["hd"]),
        mesh=mesh,
        in_specs=(
            P("grp", "ev", "hd"),
            P("grp", "ev", "hd"),
            P("grp"),
            P("grp", "ev", "hd"),
            P("grp", "ev", "hd"),
            P(None, "hd"),
            P(None, "hd"),
            P("hd"),
            P(("grp", "ev"), "hd"),
            P(("grp", "ev"), "hd"),
            P("hd"),
            P(("grp", "ev")),
            P("grp"),
        ),
        out_specs=(P("grp", "ev", "hd"), P(("grp", "ev"), "hd")),
        check_vma=False,
    )
```

```python
import jax
import jax.numpy as jnp
from jax import lax
from jax.experimental import pallas as pl
from jax.experimental.pallas import tpu as pltpu
from jax.sharding import PartitionSpec as P


HEAD = 128
BLOCK = 128
EPSILON = 1e-05
SCALE = HEAD ** (-0.5)
HALF = 0.5 * SCALE
BF16 = jnp.bfloat16
F32 = jnp.float32
ANY = pl.BlockSpec(memory_space=pl.ANY)
SMALL = pltpu.CompilerParams(vmem_limit_bytes=12 << 20)
LARGE = pltpu.CompilerParams(vmem_limit_bytes=20 << 20)


def qk(q, k):
    return lax.dot_general(q, k, (((1,), (1,)), ((), ())), preferred_element_type=F32)


def head_norm(values, gain):
    centre = jnp.mean(values, axis=-1, keepdims=True)
    shifted = values - centre
    spread = jnp.mean(shifted * shifted, axis=-1, keepdims=True)
    return shifted * lax.rsqrt(spread + EPSILON) * gain


def swap(x, axis, size, j):
    return lax.ppermute(x, axis, [(i, i ^ j) for i in range(size)])


def full(shape):
    return pl.BlockSpec(shape, lambda *_: (0,) * len(shape))


def attend(first_user, counts, half_rows, start, queries, own_first, hist_len, place, keys, values, after, resident=True):
    n = len(queries)
    width = queries[0][0].shape[2]
    hist_rows = keys.shape[1]
    users = len(counts)
    take = max(counts)
    total = sum(counts) * half_rows
    n_after = len(after)

    def kern(len_ref, place_ref, *refs):
        q_refs, k_ref, v_ref = refs[:n], refs[n], refs[n + 1]
        o_refs = refs[n + 2 + n_after :]
        for g in range(users):
            rows = counts[g] * half_rows
            at = sum(counts[:g]) * half_rows

            def run(g=g, rows=rows, at=at):
                left = len_ref[first_user + g] - place_ref[0] * hist_rows

                @pl.when(left > 0)
                def _():
                    q = [r[0, :rows, :] for r in q_refs]
                    q = q[0] if n == 1 else jnp.concatenate(q, axis=0)
                    tile = min(hist_rows, 1024 if n * rows <= 256 else 256)
                    o = jnp.zeros((n * rows, HEAD), F32)
                    for t in range(0, hist_rows, tile):
                        row = t + lax.broadcasted_iota(jnp.int32, (tile, HEAD), 0)
                        part = (0, slice(t, t + tile), slice(None))
                        if resident:
                            head = pl.multiple_of(pl.program_id(0) * HEAD, HEAD)
                            part = (first_user + g, slice(t, t + tile), pl.ds(head, HEAD))
                        v = jnp.where(row < left, v_ref[part], jnp.zeros((tile, HEAD), BF16))
                        s = qk(q, k_ref[part])
                        w = (s + s * jnp.tanh(s * HALF)).astype(BF16)
                        o = o + jnp.dot(w, v, preferred_element_type=F32)
                    o = o * HALF
                    for m, o_ref in enumerate(o_refs):
                        o_ref[at : at + rows, :] = o[m * rows : (m + 1) * rows].astype(o_ref.dtype)

                @pl.when(left <= 0)
                def _():
                    for o_ref in o_refs:
                        o_ref[at : at + rows, :] = jnp.zeros((rows, HEAD), o_ref.dtype)

            if users == 1:
                run()
            else:
                pl.when(pl.program_id(1) == g)(run)

    def q_spec(offset):
        return pl.BlockSpec((1, take * half_rows, HEAD), lambda h, g, *_: (offset + g, start, h))

    hist = pl.BlockSpec((1, hist_rows, HEAD), lambda h, g, *_: (first_user + g, 0, h))
    if resident:
        hist = pl.BlockSpec(memory_space=pltpu.VMEM)
    kinds = [F32 if own_first and i == 0 else BF16 for i in range(n)]
    return pl.pallas_call(
        kern,
        grid_spec=pltpu.PrefetchScalarGridSpec(
            num_scalar_prefetch=2,
            grid=(width // HEAD, users),
            in_specs=[q_spec(off) for _, off in queries] + [hist, hist] + [ANY] * n_after,
            out_specs=[pl.BlockSpec((total, HEAD), lambda h, g, *_: (0, h))] * n,
        ),
        out_shape=[jax.ShapeDtypeStruct((total, width), kind) for kind in kinds],
        cost_estimate=pl.CostEstimate(
            flops=8 * n * total * hist_rows * width,
            transcendentals=n * total * hist_rows * width // HEAD,
            bytes_accessed=4 * users * hist_rows * width,
        ),
        compiler_params=LARGE,
    )(hist_len, place, *[q for q, _ in queries], keys, values, *after)


def gate_events(own, own_at, others, rows, gate_at, gain, gate):
    n = len(others)
    width = own.shape[1]

    def kern(own_ref, *refs):
        p_refs, gain_ref, gate_ref, o_ref = refs[:n], refs[n], refs[n + 1], refs[n + 2]
        for h in range(width // HEAD):
            cols = slice(h * HEAD, (h + 1) * HEAD)
            total = own_ref[:, cols]
            for p in p_refs:
                total = total + p[:, cols].astype(F32)
            o_ref[:, cols] = (
                head_norm(total, gain_ref[:, cols]) * gate_ref[:, cols].astype(F32)
            ).astype(BF16)

    def at(offset):
        return pl.BlockSpec((pl.Element(rows), pl.Element(width)), lambda i: (offset, 0))

    return pl.pallas_call(
        kern,
        grid=(1,),
        in_specs=[at(own_at)] + [full((rows, width))] * n + [full((1, width)), at(gate_at)],
        out_specs=full((rows, width)),
        out_shape=jax.ShapeDtypeStruct((rows, width), BF16),
        compiler_params=SMALL,
    )(own, *others, gain, gate)


def user_of(block, count_ref, n_users):
    end = jnp.int32(0)
    user = jnp.int32(0)
    first = jnp.int32(0)
    for u in range(n_users - 1):
        end = end + lax.shift_right_logical(count_ref[u] + (BLOCK - 1), 7)
        past = block >= end
        user = jnp.where(past, u + 1, user)
        first = jnp.where(past, end, first)
    return user, first


def project(e_refs, n_hd, sizes, col_ref, wk, wv, k_ref, v_ref, at):
    part = wk.shape[0] // n_hd
    for c, size in enumerate(sizes):
        k = jnp.zeros((size, wk.shape[1]), F32)
        v = jnp.zeros((size, wk.shape[1]), F32)
        for j in range(n_hd):
            from_row = pl.ds(pl.multiple_of((col_ref[0] ^ j) * part, part), part)
            e = e_refs[c * n_hd + j][...]
            k += jnp.dot(e, wk[from_row, :], preferred_element_type=F32)
            v += jnp.dot(e, wv[from_row, :], preferred_element_type=F32)
        k_ref[at : at + size, :] = k.astype(BF16)
        v_ref[at : at + size, :] = v.astype(BF16)
        at += size


def early_keys(chunks, column, key_weight, value_weight):
    n_hd = len(chunks[0])
    flat = [p for c in chunks for p in c]
    sizes = [c[0].shape[0] for c in chunks]
    shape = (sum(sizes), key_weight.shape[1])

    def kern(col_ref, *refs):
        project(refs[: len(flat)], n_hd, sizes, col_ref, *refs[len(flat) :], 0)

    return pl.pallas_call(
        kern,
        grid_spec=pltpu.PrefetchScalarGridSpec(
            num_scalar_prefetch=1,
            grid=(1,),
            in_specs=[full(e.shape) for e in flat] + [full(key_weight.shape)] * 2,
            out_specs=[full(shape)] * 2,
        ),
        out_shape=[jax.ShapeDtypeStruct(shape, BF16)] * 2,
        compiler_params=SMALL,
        name="early_keys",
    )(column, *flat, key_weight, value_weight)


def cand_sums(n_users, early, chunks, cands, cand_count, place, column, key_weight, value_weight):
    n = len(cands)
    n_hd = len(chunks[0])
    width = key_weight.shape[1]
    flat = [p for c in chunks for p in c]
    sizes = [c[0].shape[0] for c in chunks]
    done = early[0].shape[0]
    rows = (done + sum(sizes)) // n_users
    blocks = cands[0].shape[0] // BLOCK

    def kern(count_ref, place_ref, col_ref, *refs):
        e_refs, refs = refs[: len(flat)], refs[len(flat) :]
        wk, wv, early_k, early_v = refs[:4]
        q_refs = refs[4 : 4 + n]
        keep_ref, send_ref, k_ref, v_ref = refs[-4:]
        k_ref[:done, :] = early_k[...]
        v_ref[:done, :] = early_v[...]
        project(e_refs, n_hd, sizes, col_ref, wk, wv, k_ref, v_ref, done)
        for j in range(n):
            o_ref = send_ref if j & 1 else keep_ref
            for i in range(blocks):
                user, _ = user_of((place_ref[0] ^ j) * blocks + i, count_ref, n_users)
                rws = slice(i * BLOCK, (i + 1) * BLOCK)
                own = pl.ds(pl.multiple_of(user * rows, rows), rows)
                for h in range(width // HEAD):
                    cols = slice(h * HEAD, (h + 1) * HEAD)
                    t = qk(q_refs[j][rws, cols], k_ref[own, cols]) * HALF
                    w = (t + t * jnp.tanh(t)).astype(BF16)
                    o = jnp.dot(w, v_ref[own, cols], preferred_element_type=F32)
                    o_ref[j // 2, rws, cols] = o.astype(o_ref.dtype)

    shape = (max(n // 2, 1), blocks * BLOCK, width)
    return pl.pallas_call(
        kern,
        grid_spec=pltpu.PrefetchScalarGridSpec(
            num_scalar_prefetch=3,
            grid=(1,),
            in_specs=[full(e.shape) for e in flat]
            + [full(key_weight.shape)] * 2
            + [full(early[0].shape)] * 2
            + [full(c.shape) for c in cands],
            out_specs=[full(shape)] * 2,
            scratch_shapes=[pltpu.VMEM((rows * n_users, width), BF16)] * 2,
        ),
        out_shape=[jax.ShapeDtypeStruct(shape, F32), jax.ShapeDtypeStruct(shape, BF16)],
        compiler_params=SMALL,
        name="cand_sums",
    )(cand_count, place, column, *flat, key_weight, value_weight, *early, *cands)


def gate_cands(own, others, cand_count, place, gain, gate):
    n = 1 + len(others)
    n_users = cand_count.shape[0]
    rows, width = gate.shape

    def kern(count_ref, place_ref, *refs):
        p_refs, gain_ref, gate_ref, o_ref = refs[:n], refs[n], refs[n + 1], refs[n + 2]
        for i in range(rows // BLOCK):
            rws = slice(i * BLOCK, (i + 1) * BLOCK)
            block = place_ref[0] * (rows // BLOCK) + i
            user, first = user_of(block, count_ref, n_users)
            limit = count_ref[user] - (block - first) * BLOCK
            live = lax.broadcasted_iota(jnp.int32, (BLOCK, HEAD), 0) < limit
            for h in range(width // HEAD):
                cols = slice(h * HEAD, (h + 1) * HEAD)
                total = p_refs[0][0, rws, cols].astype(F32)
                for p in p_refs[1:]:
                    total = total + p[0, rws, cols].astype(F32)
                out = head_norm(total, gain_ref[:, cols]) * gate_ref[rws, cols].astype(F32)
                o_ref[rws, cols] = jnp.where(live, out, 0.0).astype(BF16)

    part = pl.BlockSpec((1, rows, width), lambda i, *_: (0, 0, 0))
    block = full((rows, width))
    return pl.pallas_call(
        kern,
        grid_spec=pltpu.PrefetchScalarGridSpec(
            num_scalar_prefetch=2,
            grid=(1,),
            in_specs=[part] * n + [full((1, width)), block],
            out_specs=block,
        ),
        out_shape=jax.ShapeDtypeStruct((rows, width), BF16),
        compiler_params=SMALL,
        name="gate_cands",
    )(cand_count, place, own, *others, gain, gate)


def gather_pieces(x, axis, size, skip=()):
    pieces = [x] + [None] * (size - 1)
    bit = size // 2
    while bit:
        for j in range(0, size, 2 * bit):
            if pieces[j] is not None and j + bit not in skip:
                pieces[j + bit] = swap(pieces[j], axis, size, bit)
        bit //= 2
    return pieces


def make_local(n_ev, n_hd):
    def local(
        hist_keys,
        hist_values,
        hist_len,
        new_queries,
        event_gate,
        key_weight,
        value_weight,
        event_gain,
        cand_queries,
        cand_gate,
        cand_gain,
        block_user,
        cand_count,
    ):
        n_users, rows, width = new_queries.shape
        half = rows // 2
        place = lax.axis_index("ev").astype(jnp.int32).reshape(1)
        column = lax.axis_index("hd").astype(jnp.int32).reshape(1)
        event_gain = event_gain.reshape(1, width)
        cand_gain = cand_gain.reshape(1, width)
        gates = event_gate.reshape(n_users * rows, width)
        new_in_hbm, *kv_in_hbm = [
            pltpu.with_memory_space_constraint(x, pltpu.HBM) for x in (new_queries, hist_keys, hist_values)
        ]
        early_q = gather_pieces(new_queries[:1], "ev", n_ev, skip=(1,))
        queries = gather_pieces(new_queries, "ev", n_ev)
        early_q[1] = queries[1]
        queries[0] = new_in_hbm
        cands = gather_pieces(cand_queries, "ev", n_ev)
        hist = (hist_len, place, *[pltpu.with_memory_space_constraint(x, pltpu.VMEM) for x in (hist_keys, hist_values)])

        own01 = attend(0, (2, 2), half, 0, [(new_in_hbm, 0)], True, hist_len, place, *kv_in_hbm, (), resident=False)[0]

        def reduce(own, own_at, outs, halves, gate_at):
            others = [swap(o, "ev", n_ev, j + 1) for j, o in enumerate(outs)]
            return gate_events(own, own_at * half, others, halves * half, gate_at * half, event_gain, gates)


        out0 = attend(0, (2,), half, 0, [(q, 0) for q in early_q[1:]], False, *hist, (own01,))
        out1 = attend(1, (2,), half, 0, [(q, 1) for q in queries[1:]], False, *hist, (out0[0],))
        gated0 = reduce(own01, 0, out0, 2, 0)
        out2 = attend(2, (2, 1), half, 0, [(q, 2) for q in queries], True, *hist, (gated0, out1[0]))
        gated1 = reduce(own01, 2, out1, 2, 2)
        out3 = attend(3, (1,), half, 1, [(q, 3) for q in queries], True, *hist, (gated1, out2[0]))
        gated2 = reduce(out2[0], 0, out2[1:], 3, 4)
        gated3 = reduce(out3[0], 0, out3[1:], 1, 7)
        gated = [gated0, gated1, gated2, gated3]
        all_columns = [gather_pieces(g, "hd", n_hd) for g in gated]
        early = early_keys(all_columns[:2], column, key_weight, value_weight)
        keep, send = cand_sums(
            n_users, early, all_columns[2:], cands, cand_count, place, column, key_weight, value_weight
        )
        if n_ev == 1:
            cand_out = gate_cands(keep, [], cand_count, place, cand_gain, cand_gate)
        else:
            came = swap(send, "ev", n_ev, 1)
            bit = 2
            while bit < n_ev:
                total = keep + came.astype(F32)
                keep = total[0::2]
                came = swap(total[1::2].astype(BF16), "ev", n_ev, bit)
                bit *= 2
            cand_out = gate_cands(keep, [came], cand_count, place, cand_gain, cand_gate)
        event_out = jnp.concatenate(gated, axis=0)
        return event_out.reshape(n_users, rows, width), cand_out

    return local


def solution(mesh):
    return jax.shard_map(
        make_local(mesh.shape["ev"], mesh.shape["hd"]),
        mesh=mesh,
        in_specs=(
            P("grp", "ev", "hd"),
            P("grp", "ev", "hd"),
            P("grp"),
            P("grp", "ev", "hd"),
            P("grp", "ev", "hd"),
            P(None, "hd"),
            P(None, "hd"),
            P("hd"),
            P(("grp", "ev"), "hd"),
            P(("grp", "ev"), "hd"),
            P("hd"),
            P(("grp", "ev")),
            P("grp"),
        ),
        out_specs=(P("grp", "ev", "hd"), P(("grp", "ev"), "hd")),
        check_vma=False,
    )
```

```python
import jax
import jax.numpy as jnp
from jax import lax
from jax.experimental import pallas as pl
from jax.experimental.pallas import tpu as pltpu
from jax.sharding import PartitionSpec as P


HEAD = 128
BLOCK = 128
EPSILON = 1e-05
SCALE = HEAD ** (-0.5)
HALF = 0.5 * SCALE
BF16 = jnp.bfloat16
F32 = jnp.float32
ANY = pl.BlockSpec(memory_space=pl.ANY)
SMALL = pltpu.CompilerParams(vmem_limit_bytes=12 << 20)
LARGE = pltpu.CompilerParams(vmem_limit_bytes=20 << 20)


def qk(q, k):
    return lax.dot_general(q, k, (((1,), (1,)), ((), ())), preferred_element_type=F32)


def head_norm(values, gain):
    centre = jnp.mean(values, axis=-1, keepdims=True)
    shifted = values - centre
    spread = jnp.mean(shifted * shifted, axis=-1, keepdims=True)
    return shifted * lax.rsqrt(spread + EPSILON) * gain


def swap(x, axis, size, j):
    return lax.ppermute(x, axis, [(i, i ^ j) for i in range(size)])


def full(shape):
    return pl.BlockSpec(shape, lambda *_: (0,) * len(shape))


def attend(first_user, counts, half_rows, start, queries, own_first, hist_len, place, keys, values, after=()):
    n = len(queries)
    width = queries[0].shape[2]
    hist_rows = keys.shape[1]
    users = len(counts)
    take = max(counts)
    total = sum(counts) * half_rows
    n_after = len(after)

    def kern(len_ref, place_ref, *refs):
        q_refs, k_ref, v_ref = refs[:n], refs[n], refs[n + 1]
        o_refs = refs[n + 2 + n_after :]
        for g in range(users):
            user = first_user + g
            rows = counts[g] * half_rows
            at = sum(counts[:g]) * half_rows
            left = len_ref[user] - place_ref[0] * hist_rows

            @pl.when(left > 0)
            def _(g=g, user=user, rows=rows, at=at, left=left):
                tile = min(hist_rows, 256)
                for h in range(width // HEAD):
                    cols = slice(h * HEAD, (h + 1) * HEAD)
                    q = [r[g, :rows, cols] for r in q_refs]
                    q = q[0] if n == 1 else jnp.concatenate(q, axis=0)
                    o = jnp.zeros((n * rows, HEAD), F32)
                    for t in range(0, hist_rows, tile):
                        row = t + lax.broadcasted_iota(jnp.int32, (tile, HEAD), 0)
                        v = v_ref[user, t : t + tile, cols]
                        v = jnp.where(row < left, v, jnp.zeros((tile, HEAD), BF16))
                        u = qk(q, k_ref[user, t : t + tile, cols]) * HALF
                        w = (u + u * jnp.tanh(u)).astype(BF16)
                        o = o + jnp.dot(w, v, preferred_element_type=F32)
                    for m, o_ref in enumerate(o_refs):
                        o_ref[at : at + rows, cols] = o[m * rows : (m + 1) * rows].astype(o_ref.dtype)

            @pl.when(left <= 0)
            def _(rows=rows, at=at):
                for o_ref in o_refs:
                    o_ref[at : at + rows, :] = jnp.zeros((rows, width), o_ref.dtype)

    assert first_user % users == 0
    piece = pl.BlockSpec((users, take * half_rows, width), lambda *_: (first_user // users, start, 0))
    resident = pl.BlockSpec(memory_space=pltpu.VMEM)
    kinds = [F32 if own_first and i == 0 else BF16 for i in range(n)]
    return pl.pallas_call(
        kern,
        grid_spec=pltpu.PrefetchScalarGridSpec(
            num_scalar_prefetch=2,
            grid=(1,),
            in_specs=[piece] * n + [resident, resident] + [ANY] * n_after,
            out_specs=[full((total, width))] * n,
        ),
        out_shape=[jax.ShapeDtypeStruct((total, width), kind) for kind in kinds],
        cost_estimate=pl.CostEstimate(
            flops=8 * n * total * hist_rows * width,
            transcendentals=n * total * hist_rows * width // HEAD,
            bytes_accessed=4 * users * hist_rows * width,
        ),
        compiler_params=LARGE,
    )(hist_len, place, *queries, keys, values, *after)


def gate_events(own, others, rows, gate_at, gain, gate):
    n = len(others)
    width = gate.shape[1]

    def kern(own_ref, *refs):
        p_refs, gain_ref, gate_ref, o_ref = refs[:n], refs[n], refs[n + 1], refs[n + 2]
        for h in range(width // HEAD):
            cols = slice(h * HEAD, (h + 1) * HEAD)
            total = own_ref[:, cols]
            for p in p_refs:
                total = total + p[:, cols].astype(F32)
            o_ref[:, cols] = (
                head_norm(total, gain_ref[:, cols]) * gate_ref[:, cols].astype(F32)
            ).astype(BF16)

    def at(offset):
        return pl.BlockSpec((pl.Element(rows), pl.Element(width)), lambda i: (offset, 0))

    return pl.pallas_call(
        kern,
        grid=(1,),
        in_specs=[at(offset) for _, offset in [own, *others]] + [full((1, width)), at(gate_at)],
        out_specs=full((rows, width)),
        out_shape=jax.ShapeDtypeStruct((rows, width), BF16),
        compiler_params=SMALL,
    )(*[array for array, _ in [own, *others]], gain, gate)


def user_of(block, count_ref, n_users):
    end = jnp.int32(0)
    user = jnp.int32(0)
    first = jnp.int32(0)
    for u in range(n_users - 1):
        end = end + lax.shift_right_logical(count_ref[u] + (BLOCK - 1), 7)
        past = block >= end
        user = jnp.where(past, u + 1, user)
        first = jnp.where(past, end, first)
    return user, first


def project(e_refs, n_hd, sizes, col_ref, wk, wv, k_ref, v_ref, at):
    part = wk.shape[0] // n_hd
    for c, size in enumerate(sizes):
        k = jnp.zeros((size, wk.shape[1]), F32)
        v = jnp.zeros((size, wk.shape[1]), F32)
        for j in range(n_hd):
            from_row = pl.ds(pl.multiple_of((col_ref[0] ^ j) * part, part), part)
            e = e_refs[c * n_hd + j][...]
            k += jnp.dot(e, wk[from_row, :], preferred_element_type=F32)
            v += jnp.dot(e, wv[from_row, :], preferred_element_type=F32)
        k_ref[at : at + size, :] = k.astype(BF16)
        v_ref[at : at + size, :] = v.astype(BF16)
        at += size


def early_keys(chunks, column, key_weight, value_weight):
    n_hd = len(chunks[0])
    flat = [p for c in chunks for p in c]
    sizes = [c[0].shape[0] for c in chunks]
    shape = (sum(sizes), key_weight.shape[1])

    def kern(col_ref, *refs):
        project(refs[: len(flat)], n_hd, sizes, col_ref, *refs[len(flat) :], 0)

    return pl.pallas_call(
        kern,
        grid_spec=pltpu.PrefetchScalarGridSpec(
            num_scalar_prefetch=1,
            grid=(1,),
            in_specs=[full(e.shape) for e in flat] + [full(key_weight.shape)] * 2,
            out_specs=[full(shape)] * 2,
        ),
        out_shape=[jax.ShapeDtypeStruct(shape, BF16)] * 2,
        compiler_params=SMALL,
        name="early_keys",
    )(column, *flat, key_weight, value_weight)


def cand_sums(n_users, early, chunks, cands, cand_count, place, column, key_weight, value_weight):
    n = len(cands)
    n_hd = len(chunks[0])
    width = key_weight.shape[1]
    flat = [p for c in chunks for p in c]
    sizes = [c[0].shape[0] for c in chunks]
    done = early[0].shape[0]
    rows = (done + sum(sizes)) // n_users
    blocks = cands[0].shape[0] // BLOCK

    def kern(count_ref, place_ref, col_ref, *refs):
        e_refs, refs = refs[: len(flat)], refs[len(flat) :]
        wk, wv, early_k, early_v = refs[:4]
        q_refs = refs[4 : 4 + n]
        keep_ref, send_ref, k_ref, v_ref = refs[-4:]
        k_ref[:done, :] = early_k[...]
        v_ref[:done, :] = early_v[...]
        project(e_refs, n_hd, sizes, col_ref, wk, wv, k_ref, v_ref, done)
        for j in range(n):
            o_ref = send_ref if j & 1 else keep_ref
            for i in range(blocks):
                user, _ = user_of((place_ref[0] ^ j) * blocks + i, count_ref, n_users)
                rws = slice(i * BLOCK, (i + 1) * BLOCK)
                own = pl.ds(pl.multiple_of(user * rows, rows), rows)
                for h in range(width // HEAD):
                    cols = slice(h * HEAD, (h + 1) * HEAD)
                    t = qk(q_refs[j][rws, cols], k_ref[own, cols]) * HALF
                    w = (t + t * jnp.tanh(t)).astype(BF16)
                    o = jnp.dot(w, v_ref[own, cols], preferred_element_type=F32)
                    o_ref[j // 2, rws, cols] = o.astype(o_ref.dtype)

    shape = (max(n // 2, 1), blocks * BLOCK, width)
    return pl.pallas_call(
        kern,
        grid_spec=pltpu.PrefetchScalarGridSpec(
            num_scalar_prefetch=3,
            grid=(1,),
            in_specs=[full(e.shape) for e in flat]
            + [full(key_weight.shape)] * 2
            + [full(early[0].shape)] * 2
            + [full(c.shape) for c in cands],
            out_specs=[full(shape)] * 2,
            scratch_shapes=[pltpu.VMEM((rows * n_users, width), BF16)] * 2,
        ),
        out_shape=[jax.ShapeDtypeStruct(shape, F32), jax.ShapeDtypeStruct(shape, BF16)],
        compiler_params=SMALL,
        name="cand_sums",
    )(cand_count, place, column, *flat, key_weight, value_weight, *early, *cands)


def gate_cands(own, others, cand_count, place, gain, gate):
    n = 1 + len(others)
    n_users = cand_count.shape[0]
    rows, width = gate.shape

    def kern(count_ref, place_ref, *refs):
        p_refs, gain_ref, gate_ref, o_ref = refs[:n], refs[n], refs[n + 1], refs[n + 2]
        for i in range(rows // BLOCK):
            rws = slice(i * BLOCK, (i + 1) * BLOCK)
            block = place_ref[0] * (rows // BLOCK) + i
            user, first = user_of(block, count_ref, n_users)
            limit = count_ref[user] - (block - first) * BLOCK
            live = lax.broadcasted_iota(jnp.int32, (BLOCK, HEAD), 0) < limit
            for h in range(width // HEAD):
                cols = slice(h * HEAD, (h + 1) * HEAD)
                total = p_refs[0][0, rws, cols].astype(F32)
                for p in p_refs[1:]:
                    total = total + p[0, rws, cols].astype(F32)
                out = head_norm(total, gain_ref[:, cols]) * gate_ref[rws, cols].astype(F32)
                o_ref[rws, cols] = jnp.where(live, out, 0.0).astype(BF16)

    part = pl.BlockSpec((1, rows, width), lambda i, *_: (0, 0, 0))
    block = full((rows, width))
    return pl.pallas_call(
        kern,
        grid_spec=pltpu.PrefetchScalarGridSpec(
            num_scalar_prefetch=2,
            grid=(1,),
            in_specs=[part] * n + [full((1, width)), block],
            out_specs=block,
        ),
        out_shape=jax.ShapeDtypeStruct((rows, width), BF16),
        compiler_params=SMALL,
        name="gate_cands",
    )(cand_count, place, own, *others, gain, gate)


def gather_pieces(x, axis, size):
    pieces = [x] + [None] * (size - 1)
    bit = size // 2
    while bit:
        for j in range(0, size, 2 * bit):
            pieces[j + bit] = swap(pieces[j], axis, size, bit)
        bit //= 2
    return pieces


def make_local(n_ev, n_hd):
    def local(
        hist_keys,
        hist_values,
        hist_len,
        new_queries,
        event_gate,
        key_weight,
        value_weight,
        event_gain,
        cand_queries,
        cand_gate,
        cand_gain,
        block_user,
        cand_count,
    ):
        n_users, rows, width = new_queries.shape
        half = rows // 2
        place = lax.axis_index("ev").astype(jnp.int32).reshape(1)
        column = lax.axis_index("hd").astype(jnp.int32).reshape(1)
        event_gain = event_gain.reshape(1, width)
        cand_gain = cand_gain.reshape(1, width)
        gates = event_gate.reshape(n_users * rows, width)
        queries = gather_pieces(new_queries, "ev", n_ev)
        queries[0] = pltpu.with_memory_space_constraint(new_queries, pltpu.HBM)
        cands = gather_pieces(cand_queries, "ev", n_ev)
        keys, values = [pltpu.with_memory_space_constraint(x, pltpu.VMEM) for x in (hist_keys, hist_values)]
        hist = (hist_len, place, keys, values)

        def exchange(pieces, first):
            return [swap(p, "ev", n_ev, first + j) for j, p in enumerate(pieces)]

        def gate_chunk(own, others, halves, gate_at):
            return gate_events(own, others, halves * half, gate_at * half, event_gain, gates)

        own01, *near01 = attend(0, (2, 2), half, 0, queries[:2], True, *hist)
        got01 = exchange(near01, 1)
        far0 = attend(0, (2,), half, 0, queries[2:], False, *hist, (own01,))
        far1 = attend(1, (2,), half, 0, queries[2:], False, *hist, (far0[0],))
        got0, got1 = exchange(far0, 2), exchange(far1, 2)
        gated0 = gate_chunk((own01, 0), [(x, 0) for x in got01 + got0], 2, 0)
        out2 = attend(2, (2, 1), half, 0, queries, True, *hist, (gated0, far1[0]))
        gated1 = gate_chunk((own01, rows), [(x, rows) for x in got01] + [(x, 0) for x in got1], 2, 2)
        out3 = attend(3, (1,), half, 1, queries, True, *hist, (gated1, out2[0]))
        got2, got3 = exchange(out2[1:], 1), exchange(out3[1:], 1)
        gated2 = gate_chunk((out2[0], 0), [(x, 0) for x in got2], 3, 4)
        gated3 = gate_chunk((out3[0], 0), [(x, 0) for x in got3], 1, 7)
        gated = [gated0, gated1, gated2, gated3]
        all_columns = [gather_pieces(g, "hd", n_hd) for g in gated]
        early = early_keys(all_columns[:2], column, key_weight, value_weight)
        keep, send = cand_sums(
            n_users, early, all_columns[2:], cands, cand_count, place, column, key_weight, value_weight
        )
        if n_ev == 1:
            cand_out = gate_cands(keep, [], cand_count, place, cand_gain, cand_gate)
        else:
            came = swap(send, "ev", n_ev, 1)
            bit = 2
            while bit < n_ev:
                total = keep + came.astype(F32)
                keep = total[0::2]
                came = swap(total[1::2].astype(BF16), "ev", n_ev, bit)
                bit *= 2
            cand_out = gate_cands(keep, [came], cand_count, place, cand_gain, cand_gate)
        event_out = jnp.concatenate(gated, axis=0)
        return event_out.reshape(n_users, rows, width), cand_out

    return local


def solution(mesh):
    return jax.shard_map(
        make_local(mesh.shape["ev"], mesh.shape["hd"]),
        mesh=mesh,
        in_specs=(
            P("grp", "ev", "hd"),
            P("grp", "ev", "hd"),
            P("grp"),
            P("grp", "ev", "hd"),
            P("grp", "ev", "hd"),
            P(None, "hd"),
            P(None, "hd"),
            P("hd"),
            P(("grp", "ev"), "hd"),
            P(("grp", "ev"), "hd"),
            P("hd"),
            P(("grp", "ev")),
            P("grp"),
        ),
        out_specs=(P("grp", "ev", "hd"), P(("grp", "ev"), "hd")),
        check_vma=False,
    )
```

```python
import jax
import jax.numpy as jnp
from jax import lax
from jax.experimental import pallas as pl
from jax.experimental.pallas import tpu as pltpu
from jax.sharding import PartitionSpec as P


HEAD = 128
BLOCK = 128
EPSILON = 1e-05
SCALE = HEAD ** (-0.5)
HALF = 0.5 * SCALE
BF16 = jnp.bfloat16
F32 = jnp.float32
ANY = pl.BlockSpec(memory_space=pl.ANY)
SMALL = pltpu.CompilerParams(vmem_limit_bytes=12 << 20)
LARGE = pltpu.CompilerParams(vmem_limit_bytes=20 << 20)


def qk(q, k):
    return lax.dot_general(q, k, (((1,), (1,)), ((), ())), preferred_element_type=F32)


def head_norm(values, gain):
    centre = jnp.mean(values, axis=-1, keepdims=True)
    shifted = values - centre
    spread = jnp.mean(shifted * shifted, axis=-1, keepdims=True)
    return shifted * lax.rsqrt(spread + EPSILON) * gain


def swap(x, axis, size, j):
    return lax.ppermute(x, axis, [(i, i ^ j) for i in range(size)])


def full(shape):
    return pl.BlockSpec(shape, lambda *_: (0,) * len(shape))


def weigh(q, k, v, left):
    hist_rows = k[1]
    tile = min(hist_rows, 256)
    o = jnp.zeros((q.shape[0], HEAD), F32)
    for t in range(0, hist_rows, tile):
        row = t + lax.broadcasted_iota(jnp.int32, (tile, HEAD), 0)
        some = jnp.where(row < left, v[0](t, t + tile), jnp.zeros((tile, HEAD), BF16))
        u = qk(q, k[0](t, t + tile)) * HALF
        w = (u + u * jnp.tanh(u)).astype(BF16)
        o = o + jnp.dot(w, some, preferred_element_type=F32)
    return o


def join(parts):
    return parts[0] if len(parts) == 1 else jnp.concatenate(parts, axis=0)


def attend_cost(rows, hist_rows, width, hist_bytes):
    return pl.CostEstimate(
        flops=8 * rows * hist_rows * width,
        transcendentals=rows * hist_rows * width // HEAD,
        bytes_accessed=hist_bytes,
    )


def attend_near(users, queries, hist_len, place, keys, values):
    n = len(queries)
    _, rows, width = queries[0].shape
    hist_rows = keys.shape[1]

    def kern(len_ref, place_ref, *refs):
        q_refs, k_ref, v_ref, o_refs = refs[:n], refs[n], refs[n + 1], refs[n + 2 :]
        left = len_ref[pl.program_id(1)] - place_ref[0] * hist_rows

        @pl.when(left > 0)
        def _():
            q = join([r[0] for r in q_refs])
            k = (lambda a, b: k_ref[0, a:b], hist_rows)
            v = (lambda a, b: v_ref[0, a:b], hist_rows)
            o = weigh(q, k, v, left)
            for m, o_ref in enumerate(o_refs):
                o_ref[...] = o[m * rows : (m + 1) * rows].astype(o_ref.dtype)

        @pl.when(left <= 0)
        def _():
            for o_ref in o_refs:
                o_ref[...] = jnp.zeros(o_ref.shape, o_ref.dtype)

    piece = pl.BlockSpec((1, rows, HEAD), lambda h, g, *_: (g, 0, h))
    hist = pl.BlockSpec((1, hist_rows, HEAD), lambda h, g, *_: (g, 0, h))
    return pl.pallas_call(
        kern,
        grid_spec=pltpu.PrefetchScalarGridSpec(
            num_scalar_prefetch=2,
            grid=(width // HEAD, users),
            in_specs=[piece] * n + [hist, hist],
            out_specs=[pl.BlockSpec((rows, HEAD), lambda h, g, *_: (g, h))] * n,
        ),
        out_shape=[jax.ShapeDtypeStruct((users * rows, width), BF16 if i else F32) for i in range(n)],
        cost_estimate=attend_cost(users * n * rows, hist_rows, width, 4 * users * hist_rows * width),
        compiler_params=LARGE,
    )(hist_len, place, *queries, keys, values)


def attend(first_user, counts, half_rows, start, together, queries, own_first, hist_len, place, keys, values, after):
    n = len(queries)
    width = queries[0].shape[2]
    hist_rows = keys.shape[1]
    users = len(counts)
    take = max(counts)
    total = sum(counts) * half_rows
    n_after = len(after)
    block = width if together else HEAD

    def kern(len_ref, place_ref, *refs):
        q_refs, k_ref, v_ref = refs[:n], refs[n], refs[n + 1]
        o_refs = refs[n + 2 + n_after :]
        for g in range(users):
            user = first_user + g
            rows = counts[g] * half_rows
            at = sum(counts[:g]) * half_rows
            left = len_ref[user] - place_ref[0] * hist_rows

            @pl.when(left > 0)
            def _(g=g, user=user, rows=rows, at=at, left=left):
                for h in range(block // HEAD):
                    cols = slice(h * HEAD, (h + 1) * HEAD)
                    head = cols if together else pl.ds(pl.multiple_of(pl.program_id(0) * HEAD, HEAD), HEAD)
                    q = join([r[g, :rows, cols] for r in q_refs])
                    k = (lambda a, b, head=head: k_ref[user, a:b, head], hist_rows)
                    v = (lambda a, b, head=head: v_ref[user, a:b, head], hist_rows)
                    o = weigh(q, k, v, left)
                    for m, o_ref in enumerate(o_refs):
                        o_ref[at : at + rows, cols] = o[m * rows : (m + 1) * rows].astype(o_ref.dtype)

            @pl.when(left <= 0)
            def _(rows=rows, at=at):
                for o_ref in o_refs:
                    o_ref[at : at + rows, :] = jnp.zeros((rows, block), o_ref.dtype)

    assert first_user % users == 0
    piece = pl.BlockSpec((users, take * half_rows, block), lambda h, *_: (first_user // users, start, h))
    resident = pl.BlockSpec(memory_space=pltpu.VMEM)
    kinds = [F32 if own_first and i == 0 else BF16 for i in range(n)]
    return pl.pallas_call(
        kern,
        grid_spec=pltpu.PrefetchScalarGridSpec(
            num_scalar_prefetch=2,
            grid=(width // block,),
            in_specs=[piece] * n + [resident, resident] + [ANY] * n_after,
            out_specs=[pl.BlockSpec((total, block), lambda h, *_: (0, h))] * n,
        ),
        out_shape=[jax.ShapeDtypeStruct((total, width), kind) for kind in kinds],
        cost_estimate=attend_cost(n * total, hist_rows, width, 4 * users * hist_rows * width),
        compiler_params=LARGE,
    )(hist_len, place, *queries, keys, values, *after)


def gate_events(own, others, rows, gate_at, gain, gate):
    n = len(others)
    width = gate.shape[1]

    def kern(own_ref, *refs):
        p_refs, gain_ref, gate_ref, o_ref = refs[:n], refs[n], refs[n + 1], refs[n + 2]
        for h in range(width // HEAD):
            cols = slice(h * HEAD, (h + 1) * HEAD)
            total = own_ref[:, cols]
            for p in p_refs:
                total = total + p[:, cols].astype(F32)
            o_ref[:, cols] = (
                head_norm(total, gain_ref[:, cols]) * gate_ref[:, cols].astype(F32)
            ).astype(BF16)

    def at(offset):
        return pl.BlockSpec((pl.Element(rows), pl.Element(width)), lambda i: (offset, 0))

    return pl.pallas_call(
        kern,
        grid=(1,),
        in_specs=[at(offset) for _, offset in [own, *others]] + [full((1, width)), at(gate_at)],
        out_specs=full((rows, width)),
        out_shape=jax.ShapeDtypeStruct((rows, width), BF16),
        compiler_params=SMALL,
    )(*[array for array, _ in [own, *others]], gain, gate)


def user_of(block, count_ref, n_users):
    end = jnp.int32(0)
    user = jnp.int32(0)
    first = jnp.int32(0)
    for u in range(n_users - 1):
        end = end + lax.shift_right_logical(count_ref[u] + (BLOCK - 1), 7)
        past = block >= end
        user = jnp.where(past, u + 1, user)
        first = jnp.where(past, end, first)
    return user, first


def project(e_refs, n_hd, sizes, col_ref, wk, wv, k_ref, v_ref, at):
    part = wk.shape[0] // n_hd
    for c, size in enumerate(sizes):
        k = jnp.zeros((size, wk.shape[1]), F32)
        v = jnp.zeros((size, wk.shape[1]), F32)
        for j in range(n_hd):
            from_row = pl.ds(pl.multiple_of((col_ref[0] ^ j) * part, part), part)
            e = e_refs[c * n_hd + j][...]
            k += jnp.dot(e, wk[from_row, :], preferred_element_type=F32)
            v += jnp.dot(e, wv[from_row, :], preferred_element_type=F32)
        k_ref[at : at + size, :] = k.astype(BF16)
        v_ref[at : at + size, :] = v.astype(BF16)
        at += size


def early_keys(chunks, column, key_weight, value_weight):
    n_hd = len(chunks[0])
    flat = [p for c in chunks for p in c]
    sizes = [c[0].shape[0] for c in chunks]
    shape = (sum(sizes), key_weight.shape[1])

    def kern(col_ref, *refs):
        project(refs[: len(flat)], n_hd, sizes, col_ref, *refs[len(flat) :], 0)

    return pl.pallas_call(
        kern,
        grid_spec=pltpu.PrefetchScalarGridSpec(
            num_scalar_prefetch=1,
            grid=(1,),
            in_specs=[full(e.shape) for e in flat] + [full(key_weight.shape)] * 2,
            out_specs=[full(shape)] * 2,
        ),
        out_shape=[jax.ShapeDtypeStruct(shape, BF16)] * 2,
        compiler_params=SMALL,
        name="early_keys",
    )(column, *flat, key_weight, value_weight)


def cand_sums(n_users, early, chunks, cands, cand_count, place, column, key_weight, value_weight):
    n = len(cands)
    n_hd = len(chunks[0])
    width = key_weight.shape[1]
    flat = [p for c in chunks for p in c]
    sizes = [c[0].shape[0] for c in chunks]
    done = early[0].shape[0]
    rows = (done + sum(sizes)) // n_users
    blocks = cands[0].shape[0] // BLOCK

    def kern(count_ref, place_ref, col_ref, *refs):
        e_refs, refs = refs[: len(flat)], refs[len(flat) :]
        wk, wv, early_k, early_v = refs[:4]
        q_refs = refs[4 : 4 + n]
        keep_ref, send_ref, k_ref, v_ref = refs[-4:]
        k_ref[:done, :] = early_k[...]
        v_ref[:done, :] = early_v[...]
        project(e_refs, n_hd, sizes, col_ref, wk, wv, k_ref, v_ref, done)
        for j in range(n):
            o_ref = send_ref if j & 1 else keep_ref
            for i in range(blocks):
                user, _ = user_of((place_ref[0] ^ j) * blocks + i, count_ref, n_users)
                rws = slice(i * BLOCK, (i + 1) * BLOCK)
                own = pl.ds(pl.multiple_of(user * rows, rows), rows)
                for h in range(width // HEAD):
                    cols = slice(h * HEAD, (h + 1) * HEAD)
                    t = qk(q_refs[j][rws, cols], k_ref[own, cols]) * HALF
                    w = (t + t * jnp.tanh(t)).astype(BF16)
                    o = jnp.dot(w, v_ref[own, cols], preferred_element_type=F32)
                    o_ref[j // 2, rws, cols] = o.astype(o_ref.dtype)

    shape = (max(n // 2, 1), blocks * BLOCK, width)
    return pl.pallas_call(
        kern,
        grid_spec=pltpu.PrefetchScalarGridSpec(
            num_scalar_prefetch=3,
            grid=(1,),
            in_specs=[full(e.shape) for e in flat]
            + [full(key_weight.shape)] * 2
            + [full(early[0].shape)] * 2
            + [full(c.shape) for c in cands],
            out_specs=[full(shape)] * 2,
            scratch_shapes=[pltpu.VMEM((rows * n_users, width), BF16)] * 2,
        ),
        out_shape=[jax.ShapeDtypeStruct(shape, F32), jax.ShapeDtypeStruct(shape, BF16)],
        compiler_params=SMALL,
        name="cand_sums",
    )(cand_count, place, column, *flat, key_weight, value_weight, *early, *cands)


def gate_cands(own, others, cand_count, place, gain, gate):
    n = 1 + len(others)
    n_users = cand_count.shape[0]
    rows, width = gate.shape

    def kern(count_ref, place_ref, *refs):
        p_refs, gain_ref, gate_ref, o_ref = refs[:n], refs[n], refs[n + 1], refs[n + 2]
        for i in range(rows // BLOCK):
            rws = slice(i * BLOCK, (i + 1) * BLOCK)
            block = place_ref[0] * (rows // BLOCK) + i
            user, first = user_of(block, count_ref, n_users)
            limit = count_ref[user] - (block - first) * BLOCK
            live = lax.broadcasted_iota(jnp.int32, (BLOCK, HEAD), 0) < limit
            for h in range(width // HEAD):
                cols = slice(h * HEAD, (h + 1) * HEAD)
                total = p_refs[0][0, rws, cols].astype(F32)
                for p in p_refs[1:]:
                    total = total + p[0, rws, cols].astype(F32)
                out = head_norm(total, gain_ref[:, cols]) * gate_ref[rws, cols].astype(F32)
                o_ref[rws, cols] = jnp.where(live, out, 0.0).astype(BF16)

    part = pl.BlockSpec((1, rows, width), lambda i, *_: (0, 0, 0))
    block = full((rows, width))
    return pl.pallas_call(
        kern,
        grid_spec=pltpu.PrefetchScalarGridSpec(
            num_scalar_prefetch=2,
            grid=(1,),
            in_specs=[part] * n + [full((1, width)), block],
            out_specs=block,
        ),
        out_shape=jax.ShapeDtypeStruct((rows, width), BF16),
        compiler_params=SMALL,
        name="gate_cands",
    )(cand_count, place, own, *others, gain, gate)


def gather_pieces(x, axis, size):
    pieces = [x] + [None] * (size - 1)
    bit = size // 2
    while bit:
        for j in range(0, size, 2 * bit):
            pieces[j + bit] = swap(pieces[j], axis, size, bit)
        bit //= 2
    return pieces


def make_local(n_ev, n_hd):
    def local(
        hist_keys,
        hist_values,
        hist_len,
        new_queries,
        event_gate,
        key_weight,
        value_weight,
        event_gain,
        cand_queries,
        cand_gate,
        cand_gain,
        block_user,
        cand_count,
    ):
        n_users, rows, width = new_queries.shape
        half = rows // 2
        place = lax.axis_index("ev").astype(jnp.int32).reshape(1)
        column = lax.axis_index("hd").astype(jnp.int32).reshape(1)
        event_gain = event_gain.reshape(1, width)
        cand_gain = cand_gain.reshape(1, width)
        gates = event_gate.reshape(n_users * rows, width)
        queries = gather_pieces(new_queries, "ev", n_ev)
        queries[0], *in_hbm = [
            pltpu.with_memory_space_constraint(x, pltpu.HBM) for x in (new_queries, hist_keys, hist_values)
        ]
        cands = gather_pieces(cand_queries, "ev", n_ev)
        keys, values = [pltpu.with_memory_space_constraint(x, pltpu.VMEM) for x in (hist_keys, hist_values)]
        hist = (hist_len, place, keys, values)

        def exchange(pieces, first):
            return [swap(p, "ev", n_ev, first + j) for j, p in enumerate(pieces)]

        def gate_chunk(own, others, halves, gate_at):
            return gate_events(own, others, halves * half, gate_at * half, event_gain, gates)

        own01, *near01 = attend_near(2, queries[:2], hist_len, place, *in_hbm)
        got01 = exchange(near01, 1)
        far0 = attend(0, (2,), half, 0, True, queries[2:], False, *hist, (own01,))
        far1 = attend(1, (2,), half, 0, True, queries[2:], False, *hist, (far0[0],))
        got0, got1 = exchange(far0, 2), exchange(far1, 2)
        gated0 = gate_chunk((own01, 0), [(x, 0) for x in got01 + got0], 2, 0)
        out2 = attend(2, (2, 1), half, 0, False, queries, True, *hist, (gated0, far1[0]))
        gated1 = gate_chunk((own01, rows), [(x, rows) for x in got01] + [(x, 0) for x in got1], 2, 2)
        out3 = attend(3, (1,), half, 1, True, queries, True, *hist, (gated1, out2[0]))
        got2, got3 = exchange(out2[1:], 1), exchange(out3[1:], 1)
        gated2 = gate_chunk((out2[0], 0), [(x, 0) for x in got2], 3, 4)
        gated3 = gate_chunk((out3[0], 0), [(x, 0) for x in got3], 1, 7)
        gated = [gated0, gated1, gated2, gated3]
        all_columns = [gather_pieces(g, "hd", n_hd) for g in gated]
        early = early_keys(all_columns[:2], column, key_weight, value_weight)
        keep, send = cand_sums(
            n_users, early, all_columns[2:], cands, cand_count, place, column, key_weight, value_weight
        )
        if n_ev == 1:
            cand_out = gate_cands(keep, [], cand_count, place, cand_gain, cand_gate)
        else:
            came = swap(send, "ev", n_ev, 1)
            bit = 2
            while bit < n_ev:
                total = keep + came.astype(F32)
                keep = total[0::2]
                came = swap(total[1::2].astype(BF16), "ev", n_ev, bit)
                bit *= 2
            cand_out = gate_cands(keep, [came], cand_count, place, cand_gain, cand_gate)
        event_out = jnp.concatenate(gated, axis=0)
        return event_out.reshape(n_users, rows, width), cand_out

    return local


def solution(mesh):
    return jax.shard_map(
        make_local(mesh.shape["ev"], mesh.shape["hd"]),
        mesh=mesh,
        in_specs=(
            P("grp", "ev", "hd"),
            P("grp", "ev", "hd"),
            P("grp"),
            P("grp", "ev", "hd"),
            P("grp", "ev", "hd"),
            P(None, "hd"),
            P(None, "hd"),
            P("hd"),
            P(("grp", "ev"), "hd"),
            P(("grp", "ev"), "hd"),
            P("hd"),
            P(("grp", "ev")),
            P("grp"),
        ),
        out_specs=(P("grp", "ev", "hd"), P(("grp", "ev"), "hd")),
        check_vma=False,
    )
```

```python
import jax
import jax.numpy as jnp
from jax import lax
from jax.experimental import pallas as pl
from jax.experimental.pallas import tpu as pltpu
from jax.sharding import PartitionSpec as P


HEAD = 128
BLOCK = 128
EPSILON = 1e-05
SCALE = HEAD ** (-0.5)
HALF = 0.5 * SCALE
BF16 = jnp.bfloat16
F32 = jnp.float32
ANY = pl.BlockSpec(memory_space=pl.ANY)
SMALL = pltpu.CompilerParams(vmem_limit_bytes=12 << 20)
LARGE = pltpu.CompilerParams(vmem_limit_bytes=20 << 20)


def qk(q, k):
    return lax.dot_general(q, k, (((1,), (1,)), ((), ())), preferred_element_type=F32)


def head_norm(values, gain):
    centre = jnp.mean(values, axis=-1, keepdims=True)
    shifted = values - centre
    spread = jnp.mean(shifted * shifted, axis=-1, keepdims=True)
    return shifted * lax.rsqrt(spread + EPSILON) * gain


def swap(x, axis, size, j):
    return lax.ppermute(x, axis, [(i, i ^ j) for i in range(size)])


def full(shape):
    return pl.BlockSpec(shape, lambda *_: (0,) * len(shape))


def weigh(q, k, v, left):
    hist_rows = k[1]
    tile = min(hist_rows, 256)
    o = jnp.zeros((q.shape[0], HEAD), F32)
    for t in range(0, hist_rows, tile):
        row = t + lax.broadcasted_iota(jnp.int32, (tile, HEAD), 0)
        some = jnp.where(row < left, v[0](t, t + tile), jnp.zeros((tile, HEAD), BF16))
        u = qk(q, k[0](t, t + tile)) * HALF
        w = (u + u * jnp.tanh(u)).astype(BF16)
        o = o + jnp.dot(w, some, preferred_element_type=F32)
    return o


def join(parts):
    return parts[0] if len(parts) == 1 else jnp.concatenate(parts, axis=0)


def attend_cost(rows, hist_rows, width, hist_bytes):
    return pl.CostEstimate(
        flops=8 * rows * hist_rows * width,
        transcendentals=rows * hist_rows * width // HEAD,
        bytes_accessed=hist_bytes,
    )


def attend_near(users, queries, hist_len, place, keys, values):
    n = len(queries)
    _, rows, width = queries[0].shape
    hist_rows = keys.shape[1]

    def kern(len_ref, place_ref, *refs):
        q_refs, k_ref, v_ref, o_refs = refs[:n], refs[n], refs[n + 1], refs[n + 2 :]
        left = len_ref[pl.program_id(1)] - place_ref[0] * hist_rows

        @pl.when(left > 0)
        def _():
            q = join([r[0] for r in q_refs])
            k = (lambda a, b: k_ref[0, a:b], hist_rows)
            v = (lambda a, b: v_ref[0, a:b], hist_rows)
            o = weigh(q, k, v, left)
            for m, o_ref in enumerate(o_refs):
                o_ref[...] = o[m * rows : (m + 1) * rows].astype(o_ref.dtype)

        @pl.when(left <= 0)
        def _():
            for o_ref in o_refs:
                o_ref[...] = jnp.zeros(o_ref.shape, o_ref.dtype)

    piece = pl.BlockSpec((1, rows, HEAD), lambda h, g, *_: (g, 0, h))
    hist = pl.BlockSpec((1, hist_rows, HEAD), lambda h, g, *_: (g, 0, h))
    return pl.pallas_call(
        kern,
        grid_spec=pltpu.PrefetchScalarGridSpec(
            num_scalar_prefetch=2,
            grid=(width // HEAD, users),
            in_specs=[piece] * n + [hist, hist],
            out_specs=[pl.BlockSpec((rows, HEAD), lambda h, g, *_: (g, h))] * n,
        ),
        out_shape=[jax.ShapeDtypeStruct((users * rows, width), BF16 if i else F32) for i in range(n)],
        cost_estimate=attend_cost(users * n * rows, hist_rows, width, 4 * users * hist_rows * width),
        compiler_params=LARGE,
    )(hist_len, place, *queries, keys, values)


def attend(first_user, counts, half_rows, start, together, queries, own_first, hist_len, place, keys, values, after):
    n = len(queries)
    width = queries[0].shape[2]
    hist_rows = keys.shape[1]
    users = len(counts)
    take = max(counts)
    total = sum(counts) * half_rows
    n_after = len(after)
    block = width if together else HEAD

    def kern(len_ref, place_ref, *refs):
        q_refs, k_ref, v_ref = refs[:n], refs[n], refs[n + 1]
        o_refs = refs[n + 2 + n_after :]
        for g in range(users):
            user = first_user + g
            rows = counts[g] * half_rows
            at = sum(counts[:g]) * half_rows
            left = len_ref[user] - place_ref[0] * hist_rows

            @pl.when(left > 0)
            def _(g=g, user=user, rows=rows, at=at, left=left):
                for h in range(block // HEAD):
                    cols = slice(h * HEAD, (h + 1) * HEAD)
                    head = cols if together else pl.ds(pl.multiple_of(pl.program_id(0) * HEAD, HEAD), HEAD)
                    q = join([r[g, :rows, cols] for r in q_refs])
                    k = (lambda a, b, head=head: k_ref[user, a:b, head], hist_rows)
                    v = (lambda a, b, head=head: v_ref[user, a:b, head], hist_rows)
                    o = weigh(q, k, v, left)
                    for m, o_ref in enumerate(o_refs):
                        o_ref[at : at + rows, cols] = o[m * rows : (m + 1) * rows].astype(o_ref.dtype)

            @pl.when(left <= 0)
            def _(rows=rows, at=at):
                for o_ref in o_refs:
                    o_ref[at : at + rows, :] = jnp.zeros((rows, block), o_ref.dtype)

    assert first_user % users == 0
    piece = pl.BlockSpec((users, take * half_rows, block), lambda h, *_: (first_user // users, start, h))
    resident = pl.BlockSpec(memory_space=pltpu.VMEM)
    kinds = [F32 if own_first and i == 0 else BF16 for i in range(n)]
    return pl.pallas_call(
        kern,
        grid_spec=pltpu.PrefetchScalarGridSpec(
            num_scalar_prefetch=2,
            grid=(width // block,),
            in_specs=[piece] * n + [resident, resident] + [ANY] * n_after,
            out_specs=[pl.BlockSpec((total, block), lambda h, *_: (0, h))] * n,
        ),
        out_shape=[jax.ShapeDtypeStruct((total, width), kind) for kind in kinds],
        cost_estimate=attend_cost(n * total, hist_rows, width, 4 * users * hist_rows * width),
        compiler_params=LARGE,
    )(hist_len, place, *queries, keys, values, *after)


def gate_events(own, others, rows, gate_at, gain, gate):
    n = len(others)
    width = gate.shape[1]

    def kern(own_ref, *refs):
        p_refs, gain_ref, gate_ref, o_ref = refs[:n], refs[n], refs[n + 1], refs[n + 2]
        for h in range(width // HEAD):
            cols = slice(h * HEAD, (h + 1) * HEAD)
            total = own_ref[:, cols]
            for p in p_refs:
                total = total + p[:, cols].astype(F32)
            o_ref[:, cols] = (
                head_norm(total, gain_ref[:, cols]) * gate_ref[:, cols].astype(F32)
            ).astype(BF16)

    def at(offset):
        return pl.BlockSpec((pl.Element(rows), pl.Element(width)), lambda i: (offset, 0))

    return pl.pallas_call(
        kern,
        grid=(1,),
        in_specs=[at(offset) for _, offset in [own, *others]] + [full((1, width)), at(gate_at)],
        out_specs=full((rows, width)),
        out_shape=jax.ShapeDtypeStruct((rows, width), BF16),
        compiler_params=SMALL,
    )(*[array for array, _ in [own, *others]], gain, gate)


def user_of(block, count_ref, n_users):
    end = jnp.int32(0)
    user = jnp.int32(0)
    first = jnp.int32(0)
    for u in range(n_users - 1):
        end = end + lax.shift_right_logical(count_ref[u] + (BLOCK - 1), 7)
        past = block >= end
        user = jnp.where(past, u + 1, user)
        first = jnp.where(past, end, first)
    return user, first


def project(e_refs, n_hd, sizes, col_ref, wk, wv, k_ref, v_ref, at):
    part = wk.shape[0] // n_hd
    for c, size in enumerate(sizes):
        k = jnp.zeros((size, wk.shape[1]), F32)
        v = jnp.zeros((size, wk.shape[1]), F32)
        for j in range(n_hd):
            from_row = pl.ds(pl.multiple_of((col_ref[0] ^ j) * part, part), part)
            e = e_refs[c * n_hd + j][...]
            k += jnp.dot(e, wk[from_row, :], preferred_element_type=F32)
            v += jnp.dot(e, wv[from_row, :], preferred_element_type=F32)
        k_ref[at : at + size, :] = k.astype(BF16)
        v_ref[at : at + size, :] = v.astype(BF16)
        at += size


def early_keys(chunks, column, key_weight, value_weight):
    n_hd = len(chunks[0])
    flat = [p for c in chunks for p in c]
    sizes = [c[0].shape[0] for c in chunks]
    shape = (sum(sizes), key_weight.shape[1])

    def kern(col_ref, *refs):
        project(refs[: len(flat)], n_hd, sizes, col_ref, *refs[len(flat) :], 0)

    return pl.pallas_call(
        kern,
        grid_spec=pltpu.PrefetchScalarGridSpec(
            num_scalar_prefetch=1,
            grid=(1,),
            in_specs=[full(e.shape) for e in flat] + [full(key_weight.shape)] * 2,
            out_specs=[full(shape)] * 2,
        ),
        out_shape=[jax.ShapeDtypeStruct(shape, BF16)] * 2,
        compiler_params=SMALL,
        name="early_keys",
    )(column, *flat, key_weight, value_weight)


def late_keys(refs, early_refs, chunks, column_ref, keys_out):
    n_hd = len(chunks[0])
    sizes = [c[0].shape[0] for c in chunks]
    done = early_refs[0].shape[0]
    n_flat = n_hd * len(chunks)
    for out, early in zip(keys_out, early_refs):
        out[:done, :] = early[...]
    project(refs[:n_flat], n_hd, sizes, column_ref, *refs[n_flat : n_flat + 2], *keys_out, done)


def cand_sums(n_users, source, chunks, cands, at, cand_count, place, column, weights):
    n = len(cands)
    width = cands[0].shape[1]
    flat = [p for c in chunks for p in c]
    extra = [*flat, *weights] if chunks else []
    rows = (source[0].shape[0] + sum(c[0].shape[0] for c in chunks)) // n_users
    blocks = cands[0].shape[0] // BLOCK

    def kern(count_ref, place_ref, col_ref, *refs):
        q_refs, refs = refs[:n], refs[n:]
        o_refs = refs[len(extra) + 2 :][:n]
        k_ref, v_ref = refs[len(extra) :][:2]
        if chunks:
            keys_out = refs[-2:]
            late_keys(refs, (k_ref, v_ref), chunks, col_ref, keys_out)
            k_ref, v_ref = keys_out
        for m, j in enumerate(at):
            for i in range(blocks):
                user, _ = user_of((place_ref[0] ^ j) * blocks + i, count_ref, n_users)
                rws = slice(i * BLOCK, (i + 1) * BLOCK)
                own = pl.ds(pl.multiple_of(user * rows, rows), rows)
                for h in range(width // HEAD):
                    cols = slice(h * HEAD, (h + 1) * HEAD)
                    t = qk(q_refs[m][rws, cols], k_ref[own, cols]) * HALF
                    w = (t + t * jnp.tanh(t)).astype(BF16)
                    o = jnp.dot(w, v_ref[own, cols], preferred_element_type=F32)
                    o_refs[m][rws, cols] = o.astype(o_refs[m].dtype)

    piece = cands[0].shape
    shapes = [jax.ShapeDtypeStruct(piece, BF16 if j & 1 else F32) for j in at]
    if chunks:
        shapes += [jax.ShapeDtypeStruct((rows * n_users, width), BF16)] * 2
    operands = [*cands, *extra, *source]
    return pl.pallas_call(
        kern,
        grid_spec=pltpu.PrefetchScalarGridSpec(
            num_scalar_prefetch=3,
            grid=(1,),
            in_specs=[full(x.shape) for x in operands],
            out_specs=[full(x.shape) for x in shapes],
        ),
        out_shape=shapes,
        compiler_params=SMALL,
    )(cand_count, place, column, *operands)


def gate_cands(own, others, cand_count, place, gain, gate):
    n = 1 + len(others)
    n_users = cand_count.shape[0]
    rows, width = gate.shape

    def kern(count_ref, place_ref, *refs):
        p_refs, gain_ref, gate_ref, o_ref = refs[:n], refs[n], refs[n + 1], refs[n + 2]
        for i in range(rows // BLOCK):
            rws = slice(i * BLOCK, (i + 1) * BLOCK)
            block = place_ref[0] * (rows // BLOCK) + i
            user, first = user_of(block, count_ref, n_users)
            limit = count_ref[user] - (block - first) * BLOCK
            live = lax.broadcasted_iota(jnp.int32, (BLOCK, HEAD), 0) < limit
            for h in range(width // HEAD):
                cols = slice(h * HEAD, (h + 1) * HEAD)
                total = p_refs[0][rws, cols]
                for p in p_refs[1:]:
                    total = total + p[rws, cols].astype(F32)
                out = head_norm(total, gain_ref[:, cols]) * gate_ref[rws, cols].astype(F32)
                o_ref[rws, cols] = jnp.where(live, out, 0.0).astype(BF16)

    block = full((rows, width))
    return pl.pallas_call(
        kern,
        grid_spec=pltpu.PrefetchScalarGridSpec(
            num_scalar_prefetch=2,
            grid=(1,),
            in_specs=[block] * n + [full((1, width)), block],
            out_specs=block,
        ),
        out_shape=jax.ShapeDtypeStruct((rows, width), BF16),
        compiler_params=SMALL,
        name="gate_cands",
    )(cand_count, place, own, *others, gain, gate)


def gather_pieces(x, axis, size):
    pieces = [x] + [None] * (size - 1)
    bit = size // 2
    while bit:
        for j in range(0, size, 2 * bit):
            pieces[j + bit] = swap(pieces[j], axis, size, bit)
        bit //= 2
    return pieces


def make_local(n_ev, n_hd):
    def local(
        hist_keys,
        hist_values,
        hist_len,
        new_queries,
        event_gate,
        key_weight,
        value_weight,
        event_gain,
        cand_queries,
        cand_gate,
        cand_gain,
        block_user,
        cand_count,
    ):
        n_users, rows, width = new_queries.shape
        half = rows // 2
        place = lax.axis_index("ev").astype(jnp.int32).reshape(1)
        column = lax.axis_index("hd").astype(jnp.int32).reshape(1)
        event_gain = event_gain.reshape(1, width)
        cand_gain = cand_gain.reshape(1, width)
        gates = event_gate.reshape(n_users * rows, width)
        queries = gather_pieces(new_queries, "ev", n_ev)
        queries[0], *in_hbm = [
            pltpu.with_memory_space_constraint(x, pltpu.HBM) for x in (new_queries, hist_keys, hist_values)
        ]
        cands = gather_pieces(cand_queries, "ev", n_ev)
        keys, values = [pltpu.with_memory_space_constraint(x, pltpu.VMEM) for x in (hist_keys, hist_values)]
        hist = (hist_len, place, keys, values)

        def exchange(pieces, first):
            return [swap(p, "ev", n_ev, first + j) for j, p in enumerate(pieces)]

        def gate_chunk(own, others, halves, gate_at):
            return gate_events(own, others, halves * half, gate_at * half, event_gain, gates)

        own01, *near01 = attend_near(2, queries[:2], hist_len, place, *in_hbm)
        got01 = exchange(near01, 1)
        far0 = attend(0, (2,), half, 0, True, queries[2:], False, *hist, (own01,))
        far1 = attend(1, (2,), half, 0, True, queries[2:], False, *hist, (far0[0],))
        got0, got1 = exchange(far0, 2), exchange(far1, 2)
        gated0 = gate_chunk((own01, 0), [(x, 0) for x in got01 + got0], 2, 0)
        out2 = attend(2, (2,), half, 0, False, queries, True, *hist, (gated0, far1[0]))
        gated1 = gate_chunk((own01, rows), [(x, rows) for x in got01] + [(x, 0) for x in got1], 2, 2)
        out3 = attend(3, (2,), half, 0, False, queries, True, *hist, (gated1, out2[0]))
        got2, got3 = exchange(out2[1:], 1), exchange(out3[1:], 1)
        gated2 = gate_chunk((out2[0], 0), [(x, 0) for x in got2], 2, 4)
        gated3 = gate_chunk((out3[0], 0), [(x, 0) for x in got3], 2, 6)
        gated = [gated0, gated1, gated2, gated3]
        all_columns = [gather_pieces(g, "hd", n_hd) for g in gated]
        early = early_keys(all_columns[:2], column, key_weight, value_weight)
        weights = (key_weight, value_weight)
        near = list(range(min(2, n_ev)))
        far = list(range(2, n_ev))
        common = (cand_count, place, column, weights)
        *sums, all_keys, all_values = cand_sums(n_users, early, all_columns[2:], [cands[j] for j in far], far, *common)
        done = (all_keys, all_values)
        sums = [*cand_sums(n_users, done, [], [cands[j] for j in near], near, *common), *sums]
        held = {j: [x] for j, x in enumerate(sums)}
        bit = 1
        while bit < n_ev:
            for j in sorted(held, reverse=True):
                if j & bit:
                    first, *others = held.pop(j)
                    for x in others:
                        first = first + x.astype(F32)
                    held[j ^ bit].append(swap(first.astype(BF16), "ev", n_ev, bit))
            bit *= 2
        own, *others = held[0]
        cand_out = gate_cands(own, others, cand_count, place, cand_gain, cand_gate)
        event_out = jnp.concatenate(gated, axis=0)
        return event_out.reshape(n_users, rows, width), cand_out

    return local


def solution(mesh):
    return jax.shard_map(
        make_local(mesh.shape["ev"], mesh.shape["hd"]),
        mesh=mesh,
        in_specs=(
            P("grp", "ev", "hd"),
            P("grp", "ev", "hd"),
            P("grp"),
            P("grp", "ev", "hd"),
            P("grp", "ev", "hd"),
            P(None, "hd"),
            P(None, "hd"),
            P("hd"),
            P(("grp", "ev"), "hd"),
            P(("grp", "ev"), "hd"),
            P("hd"),
            P(("grp", "ev")),
            P("grp"),
        ),
        out_specs=(P("grp", "ev", "hd"), P(("grp", "ev"), "hd")),
        check_vma=False,
    )
```

```python
import jax
import jax.numpy as jnp
from jax import lax
from jax.experimental import pallas as pl
from jax.experimental.pallas import tpu as pltpu
from jax.sharding import PartitionSpec as P


HEAD = 128
BLOCK = 128
EPSILON = 1e-05
SCALE = HEAD ** (-0.5)
HALF = 0.5 * SCALE
BF16 = jnp.bfloat16
F32 = jnp.float32
ANY = pl.BlockSpec(memory_space=pl.ANY)
INSIDE = pl.BlockSpec(memory_space=pltpu.VMEM)
SMALL = pltpu.CompilerParams(vmem_limit_bytes=12 << 20)
LARGE = pltpu.CompilerParams(vmem_limit_bytes=20 << 20)


def qk(q, k):
    return lax.dot_general(q, k, (((1,), (1,)), ((), ())), preferred_element_type=F32)


def head_norm(values, gain):
    centre = jnp.mean(values, axis=-1, keepdims=True)
    shifted = values - centre
    spread = jnp.mean(shifted * shifted, axis=-1, keepdims=True)
    return shifted * lax.rsqrt(spread + EPSILON) * gain


def swap(x, axis, size, j):
    return lax.ppermute(x, axis, [(i, i ^ j) for i in range(size)])


def full(shape):
    return pl.BlockSpec(shape, lambda *_: (0,) * len(shape))


def weigh(q, k, v, left):
    hist_rows = k[1]
    tile = min(hist_rows, 256)
    o = jnp.zeros((q.shape[0], HEAD), F32)
    for t in range(0, hist_rows, tile):
        row = t + lax.broadcasted_iota(jnp.int32, (tile, HEAD), 0)
        some = jnp.where(row < left, v[0](t, t + tile), jnp.zeros((tile, HEAD), BF16))
        u = qk(q, k[0](t, t + tile)) * HALF
        w = (u + u * jnp.tanh(u)).astype(BF16)
        o = o + jnp.dot(w, some, preferred_element_type=F32)
    return o


def join(parts):
    return parts[0] if len(parts) == 1 else jnp.concatenate(parts, axis=0)


def attend_cost(rows, hist_rows, width, hist_bytes):
    return pl.CostEstimate(
        flops=8 * rows * hist_rows * width,
        transcendentals=rows * hist_rows * width // HEAD,
        bytes_accessed=hist_bytes,
    )


def attend_near(users, queries, hist_len, place, keys, values):
    n = len(queries)
    _, rows, width = queries[0].shape
    hist_rows = keys.shape[1]

    def kern(len_ref, place_ref, *refs):
        q_refs, k_ref, v_ref, o_refs = refs[:n], refs[n], refs[n + 1], refs[n + 2 :]
        left = len_ref[pl.program_id(1)] - place_ref[0] * hist_rows

        @pl.when(left > 0)
        def _():
            q = join([r[0] for r in q_refs])
            k = (lambda a, b: k_ref[0, a:b], hist_rows)
            v = (lambda a, b: v_ref[0, a:b], hist_rows)
            o = weigh(q, k, v, left)
            for m, o_ref in enumerate(o_refs):
                o_ref[...] = o[m * rows : (m + 1) * rows].astype(o_ref.dtype)

        @pl.when(left <= 0)
        def _():
            for o_ref in o_refs:
                o_ref[...] = jnp.zeros(o_ref.shape, o_ref.dtype)

    piece = pl.BlockSpec((1, rows, HEAD), lambda h, g, *_: (g, 0, h))
    hist = pl.BlockSpec((1, hist_rows, HEAD), lambda h, g, *_: (g, 0, h))
    return pl.pallas_call(
        kern,
        grid_spec=pltpu.PrefetchScalarGridSpec(
            num_scalar_prefetch=2,
            grid=(width // HEAD, users),
            in_specs=[piece] * n + [hist, hist],
            out_specs=[pl.BlockSpec((rows, HEAD), lambda h, g, *_: (g, h))] * n,
        ),
        out_shape=[jax.ShapeDtypeStruct((users * rows, width), BF16 if i else F32) for i in range(n)],
        cost_estimate=attend_cost(users * n * rows, hist_rows, width, 4 * users * hist_rows * width),
        compiler_params=LARGE,
    )(hist_len, place, *queries, keys, values)


def attend(user, heads, queries, own_first, hist_len, place, keys, values, after, earlier=(), looped=False):
    n = len(queries)
    _, rows, width = queries[0].shape
    hist_rows = keys.shape[1]
    n_after = len(after) + len(earlier)
    block = HEAD if looped else len(heads) * HEAD
    at = heads[0] * HEAD // block

    def kern(len_ref, place_ref, *refs):
        q_refs, k_ref, v_ref = refs[:n], refs[n], refs[n + 1]
        o_refs = refs[n + 2 + n_after :]
        left = len_ref[user] - place_ref[0] * hist_rows

        @pl.when(left > 0)
        def _():
            for m in range(block // HEAD):
                cols = slice(m * HEAD, (m + 1) * HEAD)
                head = slice((heads[0] + m) * HEAD, (heads[0] + m + 1) * HEAD)
                if looped:
                    head = pl.ds(pl.multiple_of((heads[0] + pl.program_id(0)) * HEAD, HEAD), HEAD)
                k = (lambda a, b, head=head: k_ref[user, a:b, head], hist_rows)
                v = (lambda a, b, head=head: v_ref[user, a:b, head], hist_rows)
                o = weigh(join([r[0, :, cols] for r in q_refs]), k, v, left)
                for i, o_ref in enumerate(o_refs):
                    o_ref[:, cols] = o[i * rows : (i + 1) * rows].astype(o_ref.dtype)

        @pl.when(left <= 0)
        def _():
            for o_ref in o_refs:
                o_ref[...] = jnp.zeros(o_ref.shape, o_ref.dtype)

    piece = pl.BlockSpec((1, rows, block), lambda g, *_: (user, 0, at + g))
    resident = pl.BlockSpec(memory_space=pltpu.VMEM)
    kinds = [F32 if own_first and i == 0 else BF16 for i in range(n)]
    return pl.pallas_call(
        kern,
        grid_spec=pltpu.PrefetchScalarGridSpec(
            num_scalar_prefetch=2,
            grid=(len(heads) * HEAD // block,),
            in_specs=[piece] * n + [resident, resident] + [ANY] * n_after,
            out_specs=[pl.BlockSpec((rows, block), lambda g, *_: (0, at + g))] * n,
        ),
        out_shape=[jax.ShapeDtypeStruct((rows, width), kind) for kind in kinds],
        input_output_aliases={4 + n + i: i for i in range(len(earlier))},
        cost_estimate=attend_cost(n * rows, hist_rows, len(heads) * HEAD, 4 * hist_rows * len(heads) * HEAD),
        compiler_params=LARGE,
    )(hist_len, place, *queries, keys, values, *earlier, *after)


def gate_events(own, others, rows, gate_at, gain, gate):
    n = len(others)
    width = gate.shape[1]

    def kern(own_ref, *refs):
        p_refs, gain_ref, gate_ref, o_ref = refs[:n], refs[n], refs[n + 1], refs[n + 2]
        for h in range(width // HEAD):
            cols = slice(h * HEAD, (h + 1) * HEAD)
            total = own_ref[:, cols]
            for p in p_refs:
                total = total + p[:, cols].astype(F32)
            o_ref[:, cols] = (
                head_norm(total, gain_ref[:, cols]) * gate_ref[:, cols].astype(F32)
            ).astype(BF16)

    def at(offset):
        return pl.BlockSpec((pl.Element(rows), pl.Element(width)), lambda i: (offset, 0))

    return pl.pallas_call(
        kern,
        grid=(1,),
        in_specs=[at(offset) for _, offset in [own, *others]] + [full((1, width)), at(gate_at)],
        out_specs=full((rows, width)),
        out_shape=jax.ShapeDtypeStruct((rows, width), BF16),
        compiler_params=SMALL,
    )(*[array for array, _ in [own, *others]], gain, gate)


def user_of(block, count_ref, n_users):
    end = jnp.int32(0)
    user = jnp.int32(0)
    first = jnp.int32(0)
    for u in range(n_users - 1):
        end = end + lax.shift_right_logical(count_ref[u] + (BLOCK - 1), 7)
        past = block >= end
        user = jnp.where(past, u + 1, user)
        first = jnp.where(past, end, first)
    return user, first


def project(e_refs, n_hd, sizes, col_ref, wk, wv, k_ref, v_ref, at):
    part = wk.shape[0] // n_hd
    for c, size in enumerate(sizes):
        k = jnp.zeros((size, wk.shape[1]), F32)
        v = jnp.zeros((size, wk.shape[1]), F32)
        for j in range(n_hd):
            from_row = pl.ds(pl.multiple_of((col_ref[0] ^ j) * part, part), part)
            e = e_refs[c * n_hd + j][...]
            k += jnp.dot(e, wk[from_row, :], preferred_element_type=F32)
            v += jnp.dot(e, wv[from_row, :], preferred_element_type=F32)
        k_ref[at : at + size, :] = k.astype(BF16)
        v_ref[at : at + size, :] = v.astype(BF16)
        at += size


def early_keys(chunks, column, key_weight, value_weight):
    n_hd = len(chunks[0])
    flat = [p for c in chunks for p in c]
    sizes = [c[0].shape[0] for c in chunks]
    shape = (sum(sizes), key_weight.shape[1])

    def kern(col_ref, *refs):
        project(refs[: len(flat)], n_hd, sizes, col_ref, *refs[len(flat) :], 0)

    return pl.pallas_call(
        kern,
        grid_spec=pltpu.PrefetchScalarGridSpec(
            num_scalar_prefetch=1,
            grid=(1,),
            in_specs=[INSIDE] * (len(flat) + 2),
            out_specs=[full(shape)] * 2,
        ),
        out_shape=[jax.ShapeDtypeStruct(shape, BF16)] * 2,
        compiler_params=SMALL,
        name="early_keys",
    )(column, *flat, key_weight, value_weight)


def late_keys(refs, early_refs, chunks, column_ref, keys_out):
    n_hd = len(chunks[0])
    sizes = [c[0].shape[0] for c in chunks]
    done = early_refs[0].shape[0]
    n_flat = n_hd * len(chunks)
    for out, early in zip(keys_out, early_refs):
        out[:done, :] = early[...]
    project(refs[:n_flat], n_hd, sizes, column_ref, *refs[n_flat : n_flat + 2], *keys_out, done)


def cand_sums(n_users, source, chunks, cands, at, cand_count, place, column, weights):
    n = len(cands)
    width = cands[0].shape[1]
    flat = [p for c in chunks for p in c]
    extra = [*flat, *weights] if chunks else []
    rows = (source[0].shape[0] + sum(c[0].shape[0] for c in chunks)) // n_users
    blocks = cands[0].shape[0] // BLOCK

    def kern(count_ref, place_ref, col_ref, *refs):
        q_refs, refs = refs[:n], refs[n:]
        o_refs = refs[len(extra) + 2 :][:n]
        k_ref, v_ref = refs[len(extra) :][:2]
        if chunks:
            keys_out = refs[-2:]
            late_keys(refs, (k_ref, v_ref), chunks, col_ref, keys_out)
            k_ref, v_ref = keys_out
        for m, j in enumerate(at):
            for i in range(blocks):
                user, _ = user_of((place_ref[0] ^ j) * blocks + i, count_ref, n_users)
                rws = slice(i * BLOCK, (i + 1) * BLOCK)
                own = pl.ds(pl.multiple_of(user * rows, rows), rows)
                for h in range(width // HEAD):
                    cols = slice(h * HEAD, (h + 1) * HEAD)
                    t = qk(q_refs[m][rws, cols], k_ref[own, cols]) * HALF
                    w = (t + t * jnp.tanh(t)).astype(BF16)
                    o = jnp.dot(w, v_ref[own, cols], preferred_element_type=F32)
                    o_refs[m][rws, cols] = o.astype(o_refs[m].dtype)

    piece = cands[0].shape
    shapes = [jax.ShapeDtypeStruct(piece, BF16 if j & 1 else F32) for j in at]
    if chunks:
        shapes += [jax.ShapeDtypeStruct((rows * n_users, width), BF16)] * 2
    operands = [*cands, *extra, *source]
    return pl.pallas_call(
        kern,
        grid_spec=pltpu.PrefetchScalarGridSpec(
            num_scalar_prefetch=3,
            grid=(1,),
            in_specs=[INSIDE] * len(operands),
            out_specs=[full(x.shape) for x in shapes],
        ),
        out_shape=shapes,
        compiler_params=SMALL,
    )(cand_count, place, column, *operands)


def gate_cands(own, others, cand_count, place, gain, gate):
    n = 1 + len(others)
    n_users = cand_count.shape[0]
    rows, width = gate.shape

    def kern(count_ref, place_ref, *refs):
        p_refs, gain_ref, gate_ref, o_ref = refs[:n], refs[n], refs[n + 1], refs[n + 2]
        for i in range(rows // BLOCK):
            rws = slice(i * BLOCK, (i + 1) * BLOCK)
            block = place_ref[0] * (rows // BLOCK) + i
            user, first = user_of(block, count_ref, n_users)
            limit = count_ref[user] - (block - first) * BLOCK
            live = lax.broadcasted_iota(jnp.int32, (BLOCK, HEAD), 0) < limit
            for h in range(width // HEAD):
                cols = slice(h * HEAD, (h + 1) * HEAD)
                total = p_refs[0][rws, cols]
                for p in p_refs[1:]:
                    total = total + p[rws, cols].astype(F32)
                out = head_norm(total, gain_ref[:, cols]) * gate_ref[rws, cols].astype(F32)
                o_ref[rws, cols] = jnp.where(live, out, 0.0).astype(BF16)

    block = full((rows, width))
    return pl.pallas_call(
        kern,
        grid_spec=pltpu.PrefetchScalarGridSpec(
            num_scalar_prefetch=2,
            grid=(1,),
            in_specs=[INSIDE] * (n + 2),
            out_specs=block,
        ),
        out_shape=jax.ShapeDtypeStruct((rows, width), BF16),
        compiler_params=SMALL,
        name="gate_cands",
    )(cand_count, place, own, *others, gain, gate)


def gather_pieces(x, axis, size):
    pieces = [x] + [None] * (size - 1)
    bit = size // 2
    while bit:
        for j in range(0, size, 2 * bit):
            pieces[j + bit] = swap(pieces[j], axis, size, bit)
        bit //= 2
    return pieces


def make_local(n_ev, n_hd):
    def local(
        hist_keys,
        hist_values,
        hist_len,
        new_queries,
        event_gate,
        key_weight,
        value_weight,
        event_gain,
        cand_queries,
        cand_gate,
        cand_gain,
        block_user,
        cand_count,
    ):
        n_users, rows, width = new_queries.shape
        half = rows // 2
        place = lax.axis_index("ev").astype(jnp.int32).reshape(1)
        column = lax.axis_index("hd").astype(jnp.int32).reshape(1)
        event_gain = event_gain.reshape(1, width)
        cand_gain = cand_gain.reshape(1, width)
        gates = event_gate.reshape(n_users * rows, width)
        queries = gather_pieces(new_queries, "ev", n_ev)
        queries[0], *in_hbm = [
            pltpu.with_memory_space_constraint(x, pltpu.HBM) for x in (new_queries, hist_keys, hist_values)
        ]
        cands = gather_pieces(cand_queries, "ev", n_ev)
        keys, values = [pltpu.with_memory_space_constraint(x, pltpu.VMEM) for x in (hist_keys, hist_values)]
        hist = (hist_len, place, keys, values)

        def exchange(pieces, first):
            return [swap(p, "ev", n_ev, first + j) for j, p in enumerate(pieces)]

        def gate_chunk(own, others, halves, gate_at):
            return gate_events(own, others, halves * half, gate_at * half, event_gain, gates)

        own01, *near01 = attend_near(2, queries[:2], hist_len, place, *in_hbm)
        got01 = exchange(near01, 1)
        heads = range(width // HEAD)
        most = range((len(heads) + 1) // 2)
        rest = range(len(most), len(heads))

        def in_two(user, before, between):
            sums = attend(user, most, queries, True, *hist, before)
            middle = between(sums[0])
            if len(rest):
                sums = attend(user, rest, queries, True, *hist, (middle,), sums)
            return sums, middle

        far0 = attend(0, heads, queries[2:], False, *hist, (own01,), looped=True)
        far1 = attend(1, heads, queries[2:], False, *hist, (far0[0],), looped=True)
        got0, got1 = exchange(far0, 2), exchange(far1, 2)
        near1 = [(x, rows) for x in got01]
        gated0 = gate_chunk((own01, 0), [(x, 0) for x in got01 + got0], 2, 0)
        out2, gated1 = in_two(
            2, (gated0, far1[0]), lambda _: gate_chunk((own01, rows), near1 + [(x, 0) for x in got1], 2, 2)
        )
        got2 = exchange(out2[1:], 1)
        out3, gated2 = in_two(3, (gated1, out2[0]), lambda _: gate_chunk((out2[0], 0), [(x, 0) for x in got2], 2, 4))
        got3 = exchange(out3[1:], 1)
        gated3 = gate_chunk((out3[0], 0), [(x, 0) for x in got3], 2, 6)
        gated = [gated0, gated1, gated2, gated3]
        all_columns = [gather_pieces(g, "hd", n_hd) for g in gated]
        early = early_keys(all_columns[:2], column, key_weight, value_weight)
        weights = (key_weight, value_weight)
        near = list(range(min(2, n_ev)))
        far = list(range(2, n_ev))
        common = (cand_count, place, column, weights)
        *sums, all_keys, all_values = cand_sums(n_users, early, all_columns[2:], [cands[j] for j in far], far, *common)
        done = (all_keys, all_values)
        sums = [*cand_sums(n_users, done, [], [cands[j] for j in near], near, *common), *sums]
        held = {j: [x] for j, x in enumerate(sums)}
        bit = 1
        while bit < n_ev:
            for j in sorted(held, reverse=True):
                if j & bit:
                    first, *others = held.pop(j)
                    for x in others:
                        first = first + x.astype(F32)
                    held[j ^ bit].append(swap(first.astype(BF16), "ev", n_ev, bit))
            bit *= 2
        own, *others = held[0]
        cand_out = gate_cands(own, others, cand_count, place, cand_gain, cand_gate)
        event_out = jnp.concatenate(gated, axis=0)
        return event_out.reshape(n_users, rows, width), cand_out

    return local


def solution(mesh):
    return jax.shard_map(
        make_local(mesh.shape["ev"], mesh.shape["hd"]),
        mesh=mesh,
        in_specs=(
            P("grp", "ev", "hd"),
            P("grp", "ev", "hd"),
            P("grp"),
            P("grp", "ev", "hd"),
            P("grp", "ev", "hd"),
            P(None, "hd"),
            P(None, "hd"),
            P("hd"),
            P(("grp", "ev"), "hd"),
            P(("grp", "ev"), "hd"),
            P("hd"),
            P(("grp", "ev")),
            P("grp"),
        ),
        out_specs=(P("grp", "ev", "hd"), P(("grp", "ev"), "hd")),
        check_vma=False,
    )
```

```python
import jax
import jax.numpy as jnp
from jax import lax
from jax.experimental import pallas as pl
from jax.experimental.pallas import tpu as pltpu
from jax.sharding import PartitionSpec as P


HEAD = 128
BLOCK = 128
EPSILON = 1e-05
SCALE = HEAD ** (-0.5)
HALF = 0.5 * SCALE
BF16 = jnp.bfloat16
F32 = jnp.float32
ANY = pl.BlockSpec(memory_space=pl.ANY)
INSIDE = pl.BlockSpec(memory_space=pltpu.VMEM)
SMALL = pltpu.CompilerParams(vmem_limit_bytes=12 << 20)
LARGE = pltpu.CompilerParams(vmem_limit_bytes=20 << 20)


def qk(q, k):
    return lax.dot_general(q, k, (((1,), (1,)), ((), ())), preferred_element_type=F32)


def head_norm(values, gain):
    centre = jnp.mean(values, axis=-1, keepdims=True)
    shifted = values - centre
    spread = jnp.mean(shifted * shifted, axis=-1, keepdims=True)
    return shifted * lax.rsqrt(spread + EPSILON) * gain


def swap(x, axis, size, j):
    return lax.ppermute(x, axis, [(i, i ^ j) for i in range(size)])


def full(shape):
    return pl.BlockSpec(shape, lambda *_: (0,) * len(shape))


def weigh(q, k, v, left):
    hist_rows = k[1]
    tile = min(hist_rows, 256)
    o = jnp.zeros((q.shape[0], HEAD), F32)
    for t in range(0, hist_rows, tile):
        row = t + lax.broadcasted_iota(jnp.int32, (tile, HEAD), 0)
        some = jnp.where(row < left, v[0](t, t + tile), jnp.zeros((tile, HEAD), BF16))
        u = qk(q, k[0](t, t + tile)) * HALF
        w = (u + u * jnp.tanh(u)).astype(BF16)
        o = o + jnp.dot(w, some, preferred_element_type=F32)
    return o


def join(parts):
    return parts[0] if len(parts) == 1 else jnp.concatenate(parts, axis=0)


def attend_cost(rows, hist_rows, width, hist_bytes):
    return pl.CostEstimate(
        flops=8 * rows * hist_rows * width,
        transcendentals=rows * hist_rows * width // HEAD,
        bytes_accessed=hist_bytes,
    )


def attend_first(users, queries, own_first, resident, hist_len, place, keys, values, after=()):
    n = len(queries)
    _, rows, width = queries[0].shape
    hist_rows = keys.shape[1]

    def kern(len_ref, place_ref, *refs):
        q_refs, k_ref, v_ref, o_refs = refs[:n], refs[n], refs[n + 1], refs[n + 2 + len(after) :]
        user, head = 0, slice(None)
        if resident:
            user, head = pl.program_id(1), pl.ds(pl.multiple_of(pl.program_id(0) * HEAD, HEAD), HEAD)
        left = len_ref[pl.program_id(1)] - place_ref[0] * hist_rows

        @pl.when(left > 0)
        def _():
            q = join([r[0] for r in q_refs])
            k = (lambda a, b: k_ref[user, a:b, head], hist_rows)
            v = (lambda a, b: v_ref[user, a:b, head], hist_rows)
            o = weigh(q, k, v, left)
            for m, o_ref in enumerate(o_refs):
                o_ref[...] = o[m * rows : (m + 1) * rows].astype(o_ref.dtype)

        @pl.when(left <= 0)
        def _():
            for o_ref in o_refs:
                o_ref[...] = jnp.zeros(o_ref.shape, o_ref.dtype)

    piece = pl.BlockSpec((1, rows, HEAD), lambda h, g, *_: (g, 0, h))
    hist = INSIDE if resident else pl.BlockSpec((1, hist_rows, HEAD), lambda h, g, *_: (g, 0, h))
    return pl.pallas_call(
        kern,
        grid_spec=pltpu.PrefetchScalarGridSpec(
            num_scalar_prefetch=2,
            grid=(width // HEAD, users),
            in_specs=[piece] * n + [hist, hist] + [ANY] * len(after),
            out_specs=[pl.BlockSpec((rows, HEAD), lambda h, g, *_: (g, h))] * n,
        ),
        out_shape=[jax.ShapeDtypeStruct((users * rows, width), F32 if own_first and i == 0 else BF16) for i in range(n)],
        cost_estimate=attend_cost(users * n * rows, hist_rows, width, 4 * users * hist_rows * width),
        compiler_params=LARGE,
    )(hist_len, place, *queries, keys, values, *after)


def attend(user, heads, queries, own_first, hist_len, place, keys, values, after, earlier=(), looped=False):
    n = len(queries)
    _, rows, width = queries[0].shape
    hist_rows = keys.shape[1]
    n_after = len(after) + len(earlier)
    block = HEAD if looped else len(heads) * HEAD
    at = heads[0] * HEAD // block

    def kern(len_ref, place_ref, *refs):
        q_refs, k_ref, v_ref = refs[:n], refs[n], refs[n + 1]
        o_refs = refs[n + 2 + n_after :]
        left = len_ref[user] - place_ref[0] * hist_rows

        @pl.when(left > 0)
        def _():
            for m in range(block // HEAD):
                cols = slice(m * HEAD, (m + 1) * HEAD)
                head = slice((heads[0] + m) * HEAD, (heads[0] + m + 1) * HEAD)
                if looped:
                    head = pl.ds(pl.multiple_of((heads[0] + pl.program_id(0)) * HEAD, HEAD), HEAD)
                k = (lambda a, b, head=head: k_ref[user, a:b, head], hist_rows)
                v = (lambda a, b, head=head: v_ref[user, a:b, head], hist_rows)
                o = weigh(join([r[0, :, cols] for r in q_refs]), k, v, left)
                for i, o_ref in enumerate(o_refs):
                    o_ref[:, cols] = o[i * rows : (i + 1) * rows].astype(o_ref.dtype)

        @pl.when(left <= 0)
        def _():
            for o_ref in o_refs:
                o_ref[...] = jnp.zeros(o_ref.shape, o_ref.dtype)

    piece = pl.BlockSpec((1, rows, block), lambda g, *_: (user, 0, at + g))
    resident = pl.BlockSpec(memory_space=pltpu.VMEM)
    kinds = [F32 if own_first and i == 0 else BF16 for i in range(n)]
    return pl.pallas_call(
        kern,
        grid_spec=pltpu.PrefetchScalarGridSpec(
            num_scalar_prefetch=2,
            grid=(len(heads) * HEAD // block,),
            in_specs=[piece] * n + [resident, resident] + [ANY] * n_after,
            out_specs=[pl.BlockSpec((rows, block), lambda g, *_: (0, at + g))] * n,
        ),
        out_shape=[jax.ShapeDtypeStruct((rows, width), kind) for kind in kinds],
        input_output_aliases={4 + n + i: i for i in range(len(earlier))},
        cost_estimate=attend_cost(n * rows, hist_rows, len(heads) * HEAD, 4 * hist_rows * len(heads) * HEAD),
        compiler_params=LARGE,
    )(hist_len, place, *queries, keys, values, *earlier, *after)


def gate_events(own, others, rows, gate_at, gain, gate):
    n = len(others)
    width = gate.shape[1]

    def kern(own_ref, *refs):
        p_refs, gain_ref, gate_ref, o_ref = refs[:n], refs[n], refs[n + 1], refs[n + 2]
        for h in range(width // HEAD):
            cols = slice(h * HEAD, (h + 1) * HEAD)
            total = own_ref[:, cols]
            for p in p_refs:
                total = total + p[:, cols].astype(F32)
            o_ref[:, cols] = (
                head_norm(total, gain_ref[:, cols]) * gate_ref[:, cols].astype(F32)
            ).astype(BF16)

    def at(offset):
        return pl.BlockSpec((pl.Element(rows), pl.Element(width)), lambda i: (offset, 0))

    return pl.pallas_call(
        kern,
        grid=(1,),
        in_specs=[at(offset) for _, offset in [own, *others]] + [full((1, width)), at(gate_at)],
        out_specs=full((rows, width)),
        out_shape=jax.ShapeDtypeStruct((rows, width), BF16),
        compiler_params=SMALL,
    )(*[array for array, _ in [own, *others]], gain, gate)


def user_of(block, count_ref, n_users):
    end = jnp.int32(0)
    user = jnp.int32(0)
    first = jnp.int32(0)
    for u in range(n_users - 1):
        end = end + lax.shift_right_logical(count_ref[u] + (BLOCK - 1), 7)
        past = block >= end
        user = jnp.where(past, u + 1, user)
        first = jnp.where(past, end, first)
    return user, first


def project(e_refs, n_hd, sizes, col_ref, wk, wv, k_ref, v_ref, at):
    part = wk.shape[0] // n_hd
    for c, size in enumerate(sizes):
        k = jnp.zeros((size, wk.shape[1]), F32)
        v = jnp.zeros((size, wk.shape[1]), F32)
        for j in range(n_hd):
            from_row = pl.ds(pl.multiple_of((col_ref[0] ^ j) * part, part), part)
            e = e_refs[c * n_hd + j][...]
            k += jnp.dot(e, wk[from_row, :], preferred_element_type=F32)
            v += jnp.dot(e, wv[from_row, :], preferred_element_type=F32)
        k_ref[at : at + size, :] = k.astype(BF16)
        v_ref[at : at + size, :] = v.astype(BF16)
        at += size


def early_keys(chunks, column, key_weight, value_weight):
    n_hd = len(chunks[0])
    flat = [p for c in chunks for p in c]
    sizes = [c[0].shape[0] for c in chunks]
    shape = (sum(sizes), key_weight.shape[1])

    def kern(col_ref, *refs):
        project(refs[: len(flat)], n_hd, sizes, col_ref, *refs[len(flat) :], 0)

    return pl.pallas_call(
        kern,
        grid_spec=pltpu.PrefetchScalarGridSpec(
            num_scalar_prefetch=1,
            grid=(1,),
            in_specs=[INSIDE] * (len(flat) + 2),
            out_specs=[full(shape)] * 2,
        ),
        out_shape=[jax.ShapeDtypeStruct(shape, BF16)] * 2,
        compiler_params=SMALL,
        name="early_keys",
    )(column, *flat, key_weight, value_weight)


def late_keys(refs, early_refs, chunks, column_ref, keys_out):
    n_hd = len(chunks[0])
    sizes = [c[0].shape[0] for c in chunks]
    done = early_refs[0].shape[0]
    n_flat = n_hd * len(chunks)
    for out, early in zip(keys_out, early_refs):
        out[:done, :] = early[...]
    project(refs[:n_flat], n_hd, sizes, column_ref, *refs[n_flat : n_flat + 2], *keys_out, done)


def cand_sums(n_users, source, chunks, cands, at, cand_count, place, column, weights):
    n = len(cands)
    width = cands[0].shape[1]
    flat = [p for c in chunks for p in c]
    extra = [*flat, *weights] if chunks else []
    rows = (source[0].shape[0] + sum(c[0].shape[0] for c in chunks)) // n_users
    blocks = cands[0].shape[0] // BLOCK

    def kern(count_ref, place_ref, col_ref, *refs):
        q_refs, refs = refs[:n], refs[n:]
        o_refs = refs[len(extra) + 2 :][:n]
        k_ref, v_ref = refs[len(extra) :][:2]
        if chunks:
            keys_out = refs[-2:]
            late_keys(refs, (k_ref, v_ref), chunks, col_ref, keys_out)
            k_ref, v_ref = keys_out
        for m, j in enumerate(at):
            for i in range(blocks):
                user, _ = user_of((place_ref[0] ^ j) * blocks + i, count_ref, n_users)
                rws = slice(i * BLOCK, (i + 1) * BLOCK)
                own = pl.ds(pl.multiple_of(user * rows, rows), rows)
                for h in range(width // HEAD):
                    cols = slice(h * HEAD, (h + 1) * HEAD)
                    t = qk(q_refs[m][rws, cols], k_ref[own, cols]) * HALF
                    w = (t + t * jnp.tanh(t)).astype(BF16)
                    o = jnp.dot(w, v_ref[own, cols], preferred_element_type=F32)
                    o_refs[m][rws, cols] = o.astype(o_refs[m].dtype)

    piece = cands[0].shape
    shapes = [jax.ShapeDtypeStruct(piece, BF16 if j & 1 else F32) for j in at]
    if chunks:
        shapes += [jax.ShapeDtypeStruct((rows * n_users, width), BF16)] * 2
    operands = [*cands, *extra, *source]
    return pl.pallas_call(
        kern,
        grid_spec=pltpu.PrefetchScalarGridSpec(
            num_scalar_prefetch=3,
            grid=(1,),
            in_specs=[INSIDE] * len(operands),
            out_specs=[full(x.shape) for x in shapes],
        ),
        out_shape=shapes,
        compiler_params=SMALL,
    )(cand_count, place, column, *operands)


def gate_cands(own, others, cand_count, place, gain, gate):
    n = 1 + len(others)
    n_users = cand_count.shape[0]
    rows, width = gate.shape

    def kern(count_ref, place_ref, *refs):
        p_refs, gain_ref, gate_ref, o_ref = refs[:n], refs[n], refs[n + 1], refs[n + 2]
        for i in range(rows // BLOCK):
            rws = slice(i * BLOCK, (i + 1) * BLOCK)
            block = place_ref[0] * (rows // BLOCK) + i
            user, first = user_of(block, count_ref, n_users)
            limit = count_ref[user] - (block - first) * BLOCK
            live = lax.broadcasted_iota(jnp.int32, (BLOCK, HEAD), 0) < limit
            for h in range(width // HEAD):
                cols = slice(h * HEAD, (h + 1) * HEAD)
                total = p_refs[0][rws, cols]
                for p in p_refs[1:]:
                    total = total + p[rws, cols].astype(F32)
                out = head_norm(total, gain_ref[:, cols]) * gate_ref[rws, cols].astype(F32)
                o_ref[rws, cols] = jnp.where(live, out, 0.0).astype(BF16)

    block = full((rows, width))
    return pl.pallas_call(
        kern,
        grid_spec=pltpu.PrefetchScalarGridSpec(
            num_scalar_prefetch=2,
            grid=(1,),
            in_specs=[INSIDE] * (n + 2),
            out_specs=block,
        ),
        out_shape=jax.ShapeDtypeStruct((rows, width), BF16),
        compiler_params=SMALL,
        name="gate_cands",
    )(cand_count, place, own, *others, gain, gate)


def gather_pieces(x, axis, size):
    pieces = [x] + [None] * (size - 1)
    bit = size // 2
    while bit:
        for j in range(0, size, 2 * bit):
            pieces[j + bit] = swap(pieces[j], axis, size, bit)
        bit //= 2
    return pieces


def make_local(n_ev, n_hd):
    def local(
        hist_keys,
        hist_values,
        hist_len,
        new_queries,
        event_gate,
        key_weight,
        value_weight,
        event_gain,
        cand_queries,
        cand_gate,
        cand_gain,
        block_user,
        cand_count,
    ):
        n_users, rows, width = new_queries.shape
        half = rows // 2
        place = lax.axis_index("ev").astype(jnp.int32).reshape(1)
        column = lax.axis_index("hd").astype(jnp.int32).reshape(1)
        event_gain = event_gain.reshape(1, width)
        cand_gain = cand_gain.reshape(1, width)
        gates = event_gate.reshape(n_users * rows, width)
        queries = gather_pieces(new_queries, "ev", n_ev)
        queries[0], *in_hbm = [
            pltpu.with_memory_space_constraint(x, pltpu.HBM) for x in (new_queries, hist_keys, hist_values)
        ]
        cands = gather_pieces(cand_queries, "ev", n_ev)
        keys, values = [pltpu.with_memory_space_constraint(x, pltpu.VMEM) for x in (hist_keys, hist_values)]
        hist = (hist_len, place, keys, values)

        def exchange(pieces, first):
            return [swap(p, "ev", n_ev, first + j) for j, p in enumerate(pieces)]

        def gate_chunk(own, others, halves, gate_at):
            return gate_events(own, others, halves * half, gate_at * half, event_gain, gates)

        heads = range(width // HEAD)
        own01, *near01 = attend_first(2, queries[:2], True, False, hist_len, place, *in_hbm)
        got01 = exchange(near01, 1)
        far01 = attend_first(2, queries[2:], False, True, *hist, (own01,))
        got01 = got01 + exchange(far01, 2)
        out2 = attend(2, heads, queries, True, *hist, (far01[0],))
        got2 = exchange(out2[1:], 1)
        gated01 = gate_chunk((own01, 0), [(x, 0) for x in got01], 4, 0)
        out3 = attend(3, heads, queries, True, *hist, (gated01, out2[0]))
        got3 = exchange(out3[1:], 1)
        gated2 = gate_chunk((out2[0], 0), [(x, 0) for x in got2], 2, 4)
        gated3 = gate_chunk((out3[0], 0), [(x, 0) for x in got3], 2, 6)
        gated = [gated01, gated2, gated3]
        all_columns = [gather_pieces(g, "hd", n_hd) for g in gated]
        early = early_keys(all_columns[:1], column, key_weight, value_weight)
        weights = (key_weight, value_weight)
        near = list(range(min(2, n_ev)))
        far = list(range(2, n_ev))
        common = (cand_count, place, column, weights)
        *sums, all_keys, all_values = cand_sums(n_users, early, all_columns[1:], [cands[j] for j in far], far, *common)
        done = (all_keys, all_values)
        sums = [*cand_sums(n_users, done, [], [cands[j] for j in near], near, *common), *sums]
        held = {j: [x] for j, x in enumerate(sums)}
        bit = 1
        while bit < n_ev:
            for j in sorted(held, reverse=True):
                if j & bit:
                    first, *others = held.pop(j)
                    for x in others:
                        first = first + x.astype(F32)
                    held[j ^ bit].append(swap(first.astype(BF16), "ev", n_ev, bit))
            bit *= 2
        own, *others = held[0]
        cand_out = gate_cands(own, others, cand_count, place, cand_gain, cand_gate)
        event_out = jnp.concatenate(gated, axis=0)
        return event_out.reshape(n_users, rows, width), cand_out

    return local


def solution(mesh):
    return jax.shard_map(
        make_local(mesh.shape["ev"], mesh.shape["hd"]),
        mesh=mesh,
        in_specs=(
            P("grp", "ev", "hd"),
            P("grp", "ev", "hd"),
            P("grp"),
            P("grp", "ev", "hd"),
            P("grp", "ev", "hd"),
            P(None, "hd"),
            P(None, "hd"),
            P("hd"),
            P(("grp", "ev"), "hd"),
            P(("grp", "ev"), "hd"),
            P("hd"),
            P(("grp", "ev")),
            P("grp"),
        ),
        out_specs=(P("grp", "ev", "hd"), P(("grp", "ev"), "hd")),
        check_vma=False,
    )
```

```python
import jax
import jax.numpy as jnp
from jax import lax
from jax.experimental import pallas as pl
from jax.experimental.pallas import tpu as pltpu
from jax.sharding import PartitionSpec as P


HEAD = 128
BLOCK = 128
EPSILON = 1e-05
SCALE = HEAD ** (-0.5)
HALF = 0.5 * SCALE
BF16 = jnp.bfloat16
F32 = jnp.float32
ANY = pl.BlockSpec(memory_space=pl.ANY)
INSIDE = pl.BlockSpec(memory_space=pltpu.VMEM)
SMALL = pltpu.CompilerParams(vmem_limit_bytes=12 << 20)
LARGE = pltpu.CompilerParams(vmem_limit_bytes=14 << 20)


def qk(q, k):
    return lax.dot_general(q, k, (((1,), (1,)), ((), ())), preferred_element_type=F32)


def head_norm(values, gain):
    centre = jnp.mean(values, axis=-1, keepdims=True)
    shifted = values - centre
    spread = jnp.mean(shifted * shifted, axis=-1, keepdims=True)
    return shifted * lax.rsqrt(spread + EPSILON) * gain


def swap(x, axis, size, j):
    return lax.ppermute(x, axis, [(i, i ^ j) for i in range(size)])


def full(shape):
    return pl.BlockSpec(shape, lambda *_: (0,) * len(shape))


def weigh(q, k, v, left):
    hist_rows = k[1]
    tile = min(hist_rows, 256)
    o = jnp.zeros((q.shape[0], HEAD), F32)
    for t in range(0, hist_rows, tile):
        row = t + lax.broadcasted_iota(jnp.int32, (tile, HEAD), 0)
        some = jnp.where(row < left, v[0](t, t + tile), jnp.zeros((tile, HEAD), BF16))
        u = qk(q, k[0](t, t + tile)) * HALF
        w = (u + u * jnp.tanh(u)).astype(BF16)
        o = o + jnp.dot(w, some, preferred_element_type=F32)
    return o


def join(parts):
    return parts[0] if len(parts) == 1 else jnp.concatenate(parts, axis=0)


def attend_cost(rows, hist_rows, width, hist_bytes):
    return pl.CostEstimate(
        flops=8 * rows * hist_rows * width,
        transcendentals=rows * hist_rows * width // HEAD,
        bytes_accessed=hist_bytes,
    )


def attend_first(users, queries, own_first, resident, hist_len, place, keys, values, after=()):
    n = len(queries)
    _, rows, width = queries[0].shape
    hist_rows = keys.shape[1]

    def kern(len_ref, place_ref, *refs):
        q_refs, k_ref, v_ref, o_refs = refs[:n], refs[n], refs[n + 1], refs[n + 2 + len(after) :]
        user, head = 0, slice(None)
        if resident:
            user, head = pl.program_id(1), pl.ds(pl.multiple_of(pl.program_id(0) * HEAD, HEAD), HEAD)
        left = len_ref[pl.program_id(1)] - place_ref[0] * hist_rows

        @pl.when(left > 0)
        def _():
            q = join([r[0] for r in q_refs])
            k = (lambda a, b: k_ref[user, a:b, head], hist_rows)
            v = (lambda a, b: v_ref[user, a:b, head], hist_rows)
            o = weigh(q, k, v, left)
            for m, o_ref in enumerate(o_refs):
                o_ref[...] = o[m * rows : (m + 1) * rows].astype(o_ref.dtype)

        @pl.when(left <= 0)
        def _():
            for o_ref in o_refs:
                o_ref[...] = jnp.zeros(o_ref.shape, o_ref.dtype)

    piece = pl.BlockSpec((1, rows, HEAD), lambda h, g, *_: (g, 0, h))
    hist = INSIDE if resident else pl.BlockSpec((1, hist_rows, HEAD), lambda h, g, *_: (g, 0, h))
    return pl.pallas_call(
        kern,
        grid_spec=pltpu.PrefetchScalarGridSpec(
            num_scalar_prefetch=2,
            grid=(width // HEAD, users),
            in_specs=[piece] * n + [hist, hist] + [ANY] * len(after),
            out_specs=[pl.BlockSpec((rows, HEAD), lambda h, g, *_: (g, h))] * n,
        ),
        out_shape=[jax.ShapeDtypeStruct((users * rows, width), F32 if own_first and i == 0 else BF16) for i in range(n)],
        cost_estimate=attend_cost(users * n * rows, hist_rows, width, 4 * users * hist_rows * width),
        compiler_params=LARGE,
    )(hist_len, place, *queries, keys, values, *after)


def attend(user, heads, queries, own_first, hist_len, place, keys, values, after, earlier=(), looped=False):
    n = len(queries)
    _, rows, width = queries[0].shape
    hist_rows = keys.shape[1]
    n_after = len(after) + len(earlier)
    block = HEAD if looped else len(heads) * HEAD
    at = heads[0] * HEAD // block

    def kern(len_ref, place_ref, *refs):
        q_refs, k_ref, v_ref = refs[:n], refs[n], refs[n + 1]
        o_refs = refs[n + 2 + n_after :]
        left = len_ref[user] - place_ref[0] * hist_rows

        @pl.when(left > 0)
        def _():
            for m in range(block // HEAD):
                cols = slice(m * HEAD, (m + 1) * HEAD)
                head = slice((heads[0] + m) * HEAD, (heads[0] + m + 1) * HEAD)
                if looped:
                    head = pl.ds(pl.multiple_of((heads[0] + pl.program_id(0)) * HEAD, HEAD), HEAD)
                k = (lambda a, b, head=head: k_ref[user, a:b, head], hist_rows)
                v = (lambda a, b, head=head: v_ref[user, a:b, head], hist_rows)
                o = weigh(join([r[0, :, cols] for r in q_refs]), k, v, left)
                for i, o_ref in enumerate(o_refs):
                    o_ref[:, cols] = o[i * rows : (i + 1) * rows].astype(o_ref.dtype)

        @pl.when(left <= 0)
        def _():
            for o_ref in o_refs:
                o_ref[...] = jnp.zeros(o_ref.shape, o_ref.dtype)

    piece = pl.BlockSpec((1, rows, block), lambda g, *_: (user, 0, at + g))
    resident = pl.BlockSpec(memory_space=pltpu.VMEM)
    kinds = [F32 if own_first and i == 0 else BF16 for i in range(n)]
    return pl.pallas_call(
        kern,
        grid_spec=pltpu.PrefetchScalarGridSpec(
            num_scalar_prefetch=2,
            grid=(len(heads) * HEAD // block,),
            in_specs=[piece] * n + [resident, resident] + [ANY] * n_after,
            out_specs=[pl.BlockSpec((rows, block), lambda g, *_: (0, at + g))] * n,
        ),
        out_shape=[jax.ShapeDtypeStruct((rows, width), kind) for kind in kinds],
        input_output_aliases={4 + n + i: i for i in range(len(earlier))},
        cost_estimate=attend_cost(n * rows, hist_rows, len(heads) * HEAD, 4 * hist_rows * len(heads) * HEAD),
        compiler_params=LARGE,
    )(hist_len, place, *queries, keys, values, *earlier, *after)


def gate_events(own, others, rows, gate_at, gain, gate):
    n = len(others)
    width = gate.shape[1]

    def kern(own_ref, *refs):
        p_refs, gain_ref, gate_ref, o_ref = refs[:n], refs[n], refs[n + 1], refs[n + 2]
        for h in range(width // HEAD):
            cols = slice(h * HEAD, (h + 1) * HEAD)
            total = own_ref[:, cols]
            for p in p_refs:
                total = total + p[:, cols].astype(F32)
            o_ref[:, cols] = (
                head_norm(total, gain_ref[:, cols]) * gate_ref[:, cols].astype(F32)
            ).astype(BF16)

    def at(offset):
        return pl.BlockSpec((pl.Element(rows), pl.Element(width)), lambda i: (offset, 0))

    return pl.pallas_call(
        kern,
        grid=(1,),
        in_specs=[at(offset) for _, offset in [own, *others]] + [full((1, width)), at(gate_at)],
        out_specs=full((rows, width)),
        out_shape=jax.ShapeDtypeStruct((rows, width), BF16),
        compiler_params=SMALL,
    )(*[array for array, _ in [own, *others]], gain, gate)


def user_of(block, count_ref, n_users):
    end = jnp.int32(0)
    user = jnp.int32(0)
    first = jnp.int32(0)
    for u in range(n_users - 1):
        end = end + lax.shift_right_logical(count_ref[u] + (BLOCK - 1), 7)
        past = block >= end
        user = jnp.where(past, u + 1, user)
        first = jnp.where(past, end, first)
    return user, first


def project(e_refs, n_hd, sizes, col_ref, wk, wv, k_ref, v_ref, at):
    part = wk.shape[0] // n_hd
    for c, size in enumerate(sizes):
        k = jnp.zeros((size, wk.shape[1]), F32)
        v = jnp.zeros((size, wk.shape[1]), F32)
        for j in range(n_hd):
            from_row = pl.ds(pl.multiple_of((col_ref[0] ^ j) * part, part), part)
            e = e_refs[c * n_hd + j][...]
            k += jnp.dot(e, wk[from_row, :], preferred_element_type=F32)
            v += jnp.dot(e, wv[from_row, :], preferred_element_type=F32)
        k_ref[at : at + size, :] = k.astype(BF16)
        v_ref[at : at + size, :] = v.astype(BF16)
        at += size


def early_keys(chunks, column, key_weight, value_weight):
    n_hd = len(chunks[0])
    flat = [p for c in chunks for p in c]
    sizes = [c[0].shape[0] for c in chunks]
    shape = (sum(sizes), key_weight.shape[1])

    def kern(col_ref, *refs):
        project(refs[: len(flat)], n_hd, sizes, col_ref, *refs[len(flat) :], 0)

    return pl.pallas_call(
        kern,
        grid_spec=pltpu.PrefetchScalarGridSpec(
            num_scalar_prefetch=1,
            grid=(1,),
            in_specs=[INSIDE] * (len(flat) + 2),
            out_specs=[full(shape)] * 2,
        ),
        out_shape=[jax.ShapeDtypeStruct(shape, BF16)] * 2,
        compiler_params=SMALL,
        name="early_keys",
    )(column, *flat, key_weight, value_weight)


def late_keys(refs, early_refs, chunks, column_ref, keys_out):
    n_hd = len(chunks[0])
    sizes = [c[0].shape[0] for c in chunks]
    done = early_refs[0].shape[0]
    n_flat = n_hd * len(chunks)
    for out, early in zip(keys_out, early_refs):
        out[:done, :] = early[...]
    project(refs[:n_flat], n_hd, sizes, column_ref, *refs[n_flat : n_flat + 2], *keys_out, done)


def cand_sums(n_users, source, chunks, cands, at, cand_count, place, column, weights):
    n = len(cands)
    width = cands[0].shape[1]
    flat = [p for c in chunks for p in c]
    extra = [*flat, *weights] if chunks else []
    rows = (source[0].shape[0] + sum(c[0].shape[0] for c in chunks)) // n_users
    blocks = cands[0].shape[0] // BLOCK

    def kern(count_ref, place_ref, col_ref, *refs):
        q_refs, refs = refs[:n], refs[n:]
        o_refs = refs[len(extra) + 2 :][:n]
        k_ref, v_ref = refs[len(extra) :][:2]
        if chunks:
            keys_out = refs[-2:]
            late_keys(refs, (k_ref, v_ref), chunks, col_ref, keys_out)
            k_ref, v_ref = keys_out
        for m, j in enumerate(at):
            for i in range(blocks):
                user, _ = user_of((place_ref[0] ^ j) * blocks + i, count_ref, n_users)
                rws = slice(i * BLOCK, (i + 1) * BLOCK)
                own = pl.ds(pl.multiple_of(user * rows, rows), rows)
                for h in range(width // HEAD):
                    cols = slice(h * HEAD, (h + 1) * HEAD)
                    t = qk(q_refs[m][rws, cols], k_ref[own, cols]) * HALF
                    w = (t + t * jnp.tanh(t)).astype(BF16)
                    o = jnp.dot(w, v_ref[own, cols], preferred_element_type=F32)
                    o_refs[m][rws, cols] = o.astype(o_refs[m].dtype)

    piece = cands[0].shape
    shapes = [jax.ShapeDtypeStruct(piece, BF16 if j & 1 else F32) for j in at]
    if chunks:
        shapes += [jax.ShapeDtypeStruct((rows * n_users, width), BF16)] * 2
    operands = [*cands, *extra, *source]
    return pl.pallas_call(
        kern,
        grid_spec=pltpu.PrefetchScalarGridSpec(
            num_scalar_prefetch=3,
            grid=(1,),
            in_specs=[INSIDE] * len(operands),
            out_specs=[full(x.shape) for x in shapes],
        ),
        out_shape=shapes,
        compiler_params=SMALL,
    )(cand_count, place, column, *operands)


def gate_cands(own, others, cand_count, place, gain, gate):
    n = 1 + len(others)
    n_users = cand_count.shape[0]
    rows, width = gate.shape

    def kern(count_ref, place_ref, *refs):
        p_refs, gain_ref, gate_ref, o_ref = refs[:n], refs[n], refs[n + 1], refs[n + 2]
        for i in range(rows // BLOCK):
            rws = slice(i * BLOCK, (i + 1) * BLOCK)
            block = place_ref[0] * (rows // BLOCK) + i
            user, first = user_of(block, count_ref, n_users)
            limit = count_ref[user] - (block - first) * BLOCK
            live = lax.broadcasted_iota(jnp.int32, (BLOCK, HEAD), 0) < limit
            for h in range(width // HEAD):
                cols = slice(h * HEAD, (h + 1) * HEAD)
                total = p_refs[0][rws, cols]
                for p in p_refs[1:]:
                    total = total + p[rws, cols].astype(F32)
                out = head_norm(total, gain_ref[:, cols]) * gate_ref[rws, cols].astype(F32)
                o_ref[rws, cols] = jnp.where(live, out, 0.0).astype(BF16)

    block = full((rows, width))
    return pl.pallas_call(
        kern,
        grid_spec=pltpu.PrefetchScalarGridSpec(
            num_scalar_prefetch=2,
            grid=(1,),
            in_specs=[INSIDE] * (n + 2),
            out_specs=block,
        ),
        out_shape=jax.ShapeDtypeStruct((rows, width), BF16),
        compiler_params=SMALL,
        name="gate_cands",
    )(cand_count, place, own, *others, gain, gate)


def gather_pieces(x, axis, size):
    pieces = [x] + [None] * (size - 1)
    bit = size // 2
    while bit:
        for j in range(0, size, 2 * bit):
            pieces[j + bit] = swap(pieces[j], axis, size, bit)
        bit //= 2
    return pieces


def make_local(n_ev, n_hd):
    def local(
        hist_keys,
        hist_values,
        hist_len,
        new_queries,
        event_gate,
        key_weight,
        value_weight,
        event_gain,
        cand_queries,
        cand_gate,
        cand_gain,
        block_user,
        cand_count,
    ):
        n_users, rows, width = new_queries.shape
        half = rows // 2
        place = lax.axis_index("ev").astype(jnp.int32).reshape(1)
        column = lax.axis_index("hd").astype(jnp.int32).reshape(1)
        event_gain = event_gain.reshape(1, width)
        cand_gain = cand_gain.reshape(1, width)
        gates = event_gate.reshape(n_users * rows, width)
        queries = gather_pieces(new_queries, "ev", n_ev)
        queries[0], *in_hbm = [
            pltpu.with_memory_space_constraint(x, pltpu.HBM) for x in (new_queries, hist_keys, hist_values)
        ]
        cands = gather_pieces(cand_queries, "ev", n_ev)
        keys, values = [pltpu.with_memory_space_constraint(x, pltpu.VMEM) for x in (hist_keys, hist_values)]
        hist = (hist_len, place, keys, values)

        def exchange(pieces, first):
            return [swap(p, "ev", n_ev, first + j) for j, p in enumerate(pieces)]

        def gate_chunk(own, others, halves, gate_at):
            return gate_events(own, others, halves * half, gate_at * half, event_gain, gates)

        heads = range(width // HEAD)
        own01, *near01 = attend_first(2, queries[:2], True, False, hist_len, place, *in_hbm)
        got01 = exchange(near01, 1)
        far01 = attend_first(2, queries[2:], False, True, *hist, (own01,))
        got01 = got01 + exchange(far01, 2)
        late = [pltpu.with_memory_space_constraint(q, pltpu.HBM) for q in queries]
        out2 = attend(2, heads, late, True, *hist, (far01[0],))
        got2 = exchange(out2[1:], 1)
        gated01 = gate_chunk((own01, 0), [(x, 0) for x in got01], 4, 0)
        out3 = attend(3, heads, late, True, *hist, (gated01, out2[0]))
        got3 = exchange(out3[1:], 1)
        gated2 = gate_chunk((out2[0], 0), [(x, 0) for x in got2], 2, 4)
        gated3 = gate_chunk((out3[0], 0), [(x, 0) for x in got3], 2, 6)
        gated = [gated01, gated2, gated3]
        all_columns = [gather_pieces(g, "hd", n_hd) for g in gated]
        early = early_keys(all_columns[:1], column, key_weight, value_weight)
        weights = (key_weight, value_weight)
        near = list(range(min(2, n_ev)))
        far = list(range(2, n_ev))
        common = (cand_count, place, column, weights)
        *sums, all_keys, all_values = cand_sums(n_users, early, all_columns[1:], [cands[j] for j in far], far, *common)
        done = (all_keys, all_values)
        sums = [*cand_sums(n_users, done, [], [cands[j] for j in near], near, *common), *sums]
        held = {j: [x] for j, x in enumerate(sums)}
        bit = 1
        while bit < n_ev:
            for j in sorted(held, reverse=True):
                if j & bit:
                    first, *others = held.pop(j)
                    for x in others:
                        first = first + x.astype(F32)
                    held[j ^ bit].append(swap(first.astype(BF16), "ev", n_ev, bit))
            bit *= 2
        own, *others = held[0]
        cand_out = gate_cands(own, others, cand_count, place, cand_gain, cand_gate)
        event_out = jnp.concatenate(gated, axis=0)
        return event_out.reshape(n_users, rows, width), cand_out

    return local


def solution(mesh):
    return jax.shard_map(
        make_local(mesh.shape["ev"], mesh.shape["hd"]),
        mesh=mesh,
        in_specs=(
            P("grp", "ev", "hd"),
            P("grp", "ev", "hd"),
            P("grp"),
            P("grp", "ev", "hd"),
            P("grp", "ev", "hd"),
            P(None, "hd"),
            P(None, "hd"),
            P("hd"),
            P(("grp", "ev"), "hd"),
            P(("grp", "ev"), "hd"),
            P("hd"),
            P(("grp", "ev")),
            P("grp"),
        ),
        out_specs=(P("grp", "ev", "hd"), P(("grp", "ev"), "hd")),
        check_vma=False,
    )
```
